512 devices in a mesh: gx: 64 (over y_hi, z, core), gy: 8 (over x, y_lo).
Axes of the slice: x: 4, y: 8 (y_hi: 4, y_lo: 2; y = y_hi * 2 + y_lo), z: 8, core: 2. Of those that a mesh axis runs over, the one named last changes fastest.
Arguments:
- fwd_pops: bfloat16 [3, 19, 256, 64, 128], P(None, None, 'gx', 'gy'), may hold values from -4 to 4
- fwd_scale: float32 [3, 256, 64, 128], P(None, 'gx', 'gy'), may hold values from 0.01 to 0.1
- seed_adjoint: float32 [19, 256, 64, 128], P(None, 'gx', 'gy'), may hold values from -16 to 16
- turbine_map: int32 [256, 64, 128], P('gx', 'gy'), may hold values from -1 to 39, as said below
- thrust: float32 [40], replicated, may hold values from 0.4 to 0.88
Outputs:
- adjoint_out: float32 [19, 256, 64, 128], P(None, 'gx', 'gy')
- thrust_grad: float32 [40], replicated
The draws below stay inside these ranges and needn't reach their ends.
Inputs may be any that keep to these rules, and one draw needn't show every extreme that they name: `turbine_map`: every turbine's disk is the set of cells in one streamwise plane within 4 cells (Euclidean, spanwise distance wrapping) of its centre; disks never intersect and every turbine covers cells.
All inputs are finite; a program needn't handle non-finite values.
Results may differ from the reference program's by a relative error of at most 0.0003.
Values sent between devices are 32-bit elements; how exact they have to be, the bound alone decides.
A program may use at most 64 MiB of HBM per device.

```python
import math
import jax
import jax.numpy as jnp
from jax import lax

CX = 4
NZ = 128
STEPS = 3
TROWS = 10
RAD = 4
NX = 256
NY = 64
TURB = 40
N_GX = 64


def draw_turbine_map(key, part):
    key_rows, key_cols, key_high = jax.random.split(jax.random.fold_in(key, 7), 3)
    columns = TURB // TROWS
    offset_rows = jax.random.randint(key_rows, (TURB,), -1, 2)
    offset_cols = jax.random.randint(key_cols, (TURB,), -2, 3)
    offset_high = jax.random.randint(key_high, (TURB,), -2, 3)
    plane_x = jnp.arange(NX, dtype=jnp.int32)[:, None, None]
    plane_y = jnp.arange(NY, dtype=jnp.int32)[None, :, None]
    plane_z = jnp.arange(NZ, dtype=jnp.int32)[None, None, :]
    result = jnp.full((NX, NY, NZ), -1, jnp.int32)
    for turbine in range(TURB):
        row_pos = turbine // columns
        col_pos = turbine % columns
        centre_x = (2 * row_pos + 1) * NX // (2 * TROWS) + offset_rows[turbine]
        centre_y = (2 * col_pos + 1) * NY // (2 * columns) + offset_cols[turbine]
        centre_z = NZ // 3 + offset_high[turbine]
        across = (plane_y - centre_y + NY // 2) % NY - NY // 2
        upward = plane_z - centre_z
        cover = (plane_x == centre_x) & (across * across + upward * upward <= RAD * RAD)
        result = jnp.where(cover, jnp.int32(turbine), result)
    return result


def block_scale(stream_key, dims, cuts, low, high):
    def one(dim, parts):
        draws = jax.random.uniform(jax.random.fold_in(jax.random.fold_in(stream_key, 6), dim), (parts,), jnp.float32, low / len(cuts), high / len(cuts))
        return jnp.repeat(jnp.exp(draws), dims[dim] // parts).reshape((-1,) + (1,) * (len(dims) - dim - 1))

    loudness = one(*cuts[0])
    for cut in cuts[1:]:
        loudness = loudness * one(*cut)
    return loudness


def gaussian(rng, dims, scale, reach, cuts=(), kind=jnp.bfloat16):
    entries = scale * jax.random.normal(rng, dims, jnp.float32)
    if cuts:
        entries = entries * block_scale(rng, dims, cuts, -0.22, 0.18)
    return jnp.clip(entries, -reach, reach).astype(kind)


def setup_inputs(seed: int = 0) -> dict:
    arg_keys = jax.random.split(jax.random.key(seed), 6)
    return {
        "fwd_pops": gaussian(arg_keys[0], (STEPS, 19, NX, NY, NZ), 1.0, 4.0, ((2, 64), (3, 8))),
        "fwd_scale": jnp.clip(jnp.exp(math.log(0.1) - 2.3025851 * jax.random.uniform(arg_keys[1], (STEPS, NX, NY, NZ), jnp.float32) ** block_scale(arg_keys[1], (STEPS, NX, NY, NZ), ((1, 64), (2, 8)), -0.2, 0.2)), 0.01, 0.1),
        "seed_adjoint": gaussian(arg_keys[2], (19, NX, NY, NZ), 4.0, 16.0, ((1, 64), (2, 8)), jnp.float32),
        "turbine_map": draw_turbine_map(jax.random.fold_in(arg_keys[5], 71), 0),
        "thrust": jnp.clip(jax.random.uniform(arg_keys[4], (TURB,), jnp.float32, 0.4, 0.88), 0.4, 0.88),
    }


VELOCITIES = ((0, 0, 0), (1, 0, 0), (-1, 0, 0), (0, 1, 0), (0, -1, 0), (0, 0, 1), (0, 0, -1), (1, 1, 0), (-1, -1, 0), (1, -1, 0), (-1, 1, 0), (1, 0, 1), (-1, 0, -1), (1, 0, -1), (-1, 0, 1), (0, 1, 1), (0, -1, -1), (0, 1, -1), (0, -1, 1))
OPPOSITE = (0, 2, 1, 4, 3, 6, 5, 8, 7, 10, 9, 12, 11, 14, 13, 16, 15, 18, 17)
WEIGHTS = tuple([1.0 / 3.0] + [1.0 / 18.0] * 6 + [1.0 / 36.0] * 12)
MEAN_FLOW = 0.1
TAU_BASE = 0.51
SMAG_COEF = 18.0 * 1.4142135623730951 * 0.17 * 0.17
QUAD_FLOOR = 0.0001
PAIRS = ((0, 0, 1.0), (1, 1, 1.0), (2, 2, 1.0), (0, 1, 2.0), (0, 2, 2.0), (1, 2, 2.0))

def base_values():
    values = []
    for member in range(19):
        along = float(VELOCITIES[member][0])
        values.append(WEIGHTS[member] * (1.0 + 3.0 * MEAN_FLOW * along + 4.5 * MEAN_FLOW * MEAN_FLOW * along * along - 1.5 * MEAN_FLOW * MEAN_FLOW))
    return values

def decode(stored, scaling):
    base = jnp.asarray(base_values(), dtype=jnp.float32)
    return base[:, None, None, None] * (1.0 + scaling[None] * stored.astype(jnp.float32))

def collide(populations, thrust_cell):
    density = populations[0]
    for member in range(1, 19):
        density = density + populations[member]
    velocity = []
    for axis_id in range(3):
        moment = jnp.zeros_like(density)
        for member in range(19):
            component = VELOCITIES[member][axis_id]
            if component != 0:
                moment = moment + float(component) * populations[member]
        velocity.append(moment / density)
    speed_sq = velocity[0] * velocity[0] + velocity[1] * velocity[1] + velocity[2] * velocity[2]
    nonequil = []
    for member in range(19):
        proj = float(VELOCITIES[member][0]) * velocity[0] + float(VELOCITIES[member][1]) * velocity[1] + float(VELOCITIES[member][2]) * velocity[2]
        equilib = WEIGHTS[member] * density * (1.0 + 3.0 * proj + 4.5 * proj * proj - 1.5 * speed_sq)
        nonequil.append(populations[member] - equilib)
    stress_sum = jnp.zeros_like(density)
    for first, second, factor in PAIRS:
        stress = jnp.zeros_like(density)
        for member in range(19):
            product = VELOCITIES[member][first] * VELOCITIES[member][second]
            if product != 0:
                stress = stress + float(product) * nonequil[member]
        stress_sum = stress_sum + factor * stress * stress
    magnitude = jnp.sqrt(stress_sum + QUAD_FLOOR)
    relaxation = 0.5 * (TAU_BASE + jnp.sqrt(TAU_BASE * TAU_BASE + SMAG_COEF * magnitude / density))
    thrust_force = -0.5 * thrust_cell * velocity[0] * jnp.abs(velocity[0])
    result = []
    for member in range(19):
        result.append(populations[member] - nonequil[member] / relaxation + 3.0 * WEIGHTS[member] * float(VELOCITIES[member][0]) * thrust_force)
    return jnp.stack(result)

def local_thrust(values):
    return 4.0 * values / jnp.square(1.0 + jnp.sqrt(1.0 - values))

def finish_vertical(shifted, adjoint):
    result = []
    for member in range(19):
        vertical = VELOCITIES[member][2]
        mirror = adjoint[OPPOSITE[member]]
        if vertical == 1:
            result.append(jnp.concatenate([shifted[member][..., 1:], mirror[..., -1:]], axis=-1))
        elif vertical == -1:
            result.append(jnp.concatenate([mirror[..., :1], shifted[member][..., :-1]], axis=-1))
        else:
            result.append(shifted[member])
    return jnp.stack(result)

def pull_plane(adjoint):
    shifted = []
    for member in range(19):
        shifted.append(jnp.roll(adjoint[member], (-VELOCITIES[member][0], -VELOCITIES[member][1]), axis=(0, 1)))
    return shifted

def block_step(inputs):
    stored, scaling, incoming, thrust_cell = inputs
    populations = decode(stored, scaling)
    _, pullback = jax.vjp(collide, populations, thrust_cell)
    return pullback(incoming)

def reference(fwd_pops, fwd_scale, seed_adjoint, turbine_map, thrust):
    inside = turbine_map >= 0
    ids = jnp.maximum(turbine_map, 0)

    def cell_thrust(values):
        return jnp.where(inside, local_thrust(values)[ids], 0.0)
    thrust_cell, thrust_pull = jax.vjp(cell_thrust, thrust)
    cell_blocks = thrust_cell.reshape(N_GX, CX, NY, NZ)
    adjoint = seed_adjoint
    accumulated = jnp.zeros((NX, NY, NZ), jnp.float32)
    for instant in range(STEPS - 1, -1, -1):
        incoming = finish_vertical(pull_plane(adjoint), adjoint)
        stored = fwd_pops[instant].reshape(19, N_GX, CX, NY, NZ).transpose(1, 0, 2, 3, 4)
        scaling = fwd_scale[instant].reshape(N_GX, CX, NY, NZ)
        moving = incoming.reshape(19, N_GX, CX, NY, NZ).transpose(1, 0, 2, 3, 4)
        new_blocks, cell_grad = lax.map(block_step, (stored, scaling, moving, cell_blocks))
        adjoint = new_blocks.transpose(1, 0, 2, 3, 4).reshape(19, NX, NY, NZ)
        accumulated = accumulated + cell_grad.reshape(NX, NY, NZ)
    thrust_grad = thrust_pull(accumulated)[0]
    return (adjoint, thrust_grad)
```

```python
import functools

import jax
import jax.numpy as jnp
from jax import lax
from jax.experimental import pallas as pl
from jax.experimental.pallas import tpu as pltpu
from jax.sharding import PartitionSpec as P

MESH = pl.DeviceIdType.MESH
F32 = jnp.float32

VELOCITIES = (
    (0, 0, 0),
    (1, 0, 0),
    (-1, 0, 0),
    (0, 1, 0),
    (0, -1, 0),
    (0, 0, 1),
    (0, 0, -1),
    (1, 1, 0),
    (-1, -1, 0),
    (1, -1, 0),
    (-1, 1, 0),
    (1, 0, 1),
    (-1, 0, -1),
    (1, 0, -1),
    (-1, 0, 1),
    (0, 1, 1),
    (0, -1, -1),
    (0, 1, -1),
    (0, -1, 1),
)
OPPOSITE = (0, 2, 1, 4, 3, 6, 5, 8, 7, 10, 9, 12, 11, 14, 13, 16, 15, 18, 17)
WEIGHTS = tuple([1.0 / 3.0] + [1.0 / 18.0] * 6 + [1.0 / 36.0] * 12)
MEAN_FLOW = 0.1
TAU_BASE = 0.51
SMAG_COEF = 18.0 * 1.4142135623730951 * 0.17 * 0.17
QUAD_FLOOR = 0.0001

SLOTS = (9, 1, 11, 13, 7, 3, 15, 17, 10, 2, 12, 14, 8, 4, 16, 18, 9, 0, 5, 6)
SLOT = {member: SLOTS.index(member) for member in range(19)}
YP = SLOTS[4:9]
YM = SLOTS[12:17]
CORES = 2
Z_CHIPS = 8
Y_LO = 2

C_N = 0
C_Q = 19
C_G = 28
C_U = 31
C_RM, C_OMB, C_W12, C_UU, C_W8, C_KX, C_KXU, C_GK = range(34, 42)
N_COEF = 42


def base_values():
    values = []
    for member in range(19):
        along = float(VELOCITIES[member][0])
        values.append(
            WEIGHTS[member]
            * (
                1.0
                + 3.0 * MEAN_FLOW * along
                + 4.5 * MEAN_FLOW * MEAN_FLOW * along * along
                - 1.5 * MEAN_FLOW * MEAN_FLOW
            )
        )
    return values


def total(terms):
    terms = list(terms)
    while len(terms) > 1:
        terms = [
            terms[i] + terms[i + 1] if i + 1 < len(terms) else terms[i]
            for i in range(0, len(terms), 2)
        ]
    return terms[0]


def second_moments(pair):
    sx, sy, sz, a, b, c, d, e, f = pair
    txy, txz, tyz = a + b, c + d, e + f
    return sx, sy, sz, txy, txz, tyz, a - b, c - d, e - f


def coefficients(pops, scale, k):
    base = base_values()
    f = [base[i] + (base[i] * scale) * pops[i] for i in range(19)]
    rho = total(f)
    sums = [f[2 * p + 1] + f[2 * p + 2] for p in range(9)]
    difs = [f[2 * p + 1] - f[2 * p + 2] for p in range(9)]
    jx = (difs[0] + difs[3] + difs[4]) + (difs[5] + difs[6])
    jy = (difs[1] + difs[3] - difs[4]) + (difs[7] + difs[8])
    jz = (difs[2] + difs[5] - difs[6]) + (difs[7] - difs[8])
    inv = 1.0 / rho
    u = (jx * inv, jy * inv, jz * inv)
    u2 = u[0] * u[0] + u[1] * u[1] + u[2] * u[2]
    rest = 1.0 - 1.5 * u2
    n = [None] * 19
    third = rho * (1.0 / 3.0)
    n[0] = f[0] - third * rest
    r18 = rho * (1.0 / 18.0)
    r36 = rho * (1.0 / 36.0)
    proj = (
        u[0],
        u[1],
        u[2],
        u[0] + u[1],
        u[0] - u[1],
        u[0] + u[2],
        u[0] - u[2],
        u[1] + u[2],
        u[1] - u[2],
    )
    for p in range(9):
        even = rest + 4.5 * (proj[p] * proj[p])
        odd = 3.0 * proj[p]
        weight = r18 if p < 3 else r36
        n[2 * p + 1] = f[2 * p + 1] - weight * (even + odd)
        n[2 * p + 2] = f[2 * p + 2] - weight * (even - odd)
    pair = [n[2 * p + 1] + n[2 * p + 2] for p in range(9)]
    sx, sy, sz, txy, txz, tyz, pxy, pxz, pyz = second_moments(pair)
    pxx = sx + txy + txz
    pyy = sy + txy + tyz
    pzz = sz + txz + tyz
    square = (pxx * pxx + pyy * pyy + pzz * pzz) + 2.0 * (
        pxy * pxy + pxz * pxz + pyz * pyz
    )
    q = jnp.sqrt(square + QUAD_FLOOR)
    s = jnp.sqrt(TAU_BASE * TAU_BASE + SMAG_COEF * (q * inv))
    om = 2.0 / (TAU_BASE + s)
    a1 = (om * om) * (0.25 * SMAG_COEF) * inv / (s * q)
    a2 = a1 * (q * q) * inv
    pu = (
        pxx * u[0] + pxy * u[1] + pxz * u[2],
        pxy * u[0] + pyy * u[1] + pyz * u[2],
        pxz * u[0] + pyz * u[1] + pzz * u[2],
    )
    upu = u[0] * pu[0] + u[1] * pu[1] + u[2] * pu[2]
    trace = pxx + pyy + pzz
    quads = (
        pxx,
        pyy,
        pzz,
        pxx + pyy + 2.0 * pxy,
        pxx + pyy - 2.0 * pxy,
        pxx + pzz + 2.0 * pxz,
        pxx + pzz - 2.0 * pxz,
        pyy + pzz + 2.0 * pyz,
        pyy + pzz - 2.0 * pyz,
    )
    absu = jnp.abs(u[0])
    kx = k * absu * inv * (1.0 / 12.0)
    out = list(n)
    out += [a1 * value for value in quads]
    out += [(2.0 * a1) * value for value in pu]
    out += list(u)
    out += [
        a2 + a1 * (trace * (1.0 / 3.0) - upu),
        1.0 - om,
        om * (1.0 / 12.0),
        om * (1.0 / 36.0) * (1.0 + 1.5 * u2),
        om * 0.125,
        kx,
        kx * u[0],
        (-1.5 / 36.0) * (u[0] * absu),
    ]
    return out


def transposed(mu, co):
    sums = [mu[2 * p + 1] + mu[2 * p + 2] for p in range(9)]
    difs = [mu[2 * p + 1] - mu[2 * p + 2] for p in range(9)]
    sx, sy, sz, txy, txz, tyz, mxy, mxz, myz = second_moments(sums)
    sx, sy, sz = sx + sx, sy + sy, sz + sz
    mxx = sx + txy + txz
    myy = sy + txy + tyz
    mzz = sz + txz + tyz
    m0 = 12.0 * mu[0] + ((sx + sy + sz) + (txy + txz + tyz))
    m1x = (difs[0] + difs[0]) + (difs[3] + difs[4]) + (difs[5] + difs[6])
    m1y = (difs[1] + difs[1]) + (difs[3] - difs[4]) + (difs[7] + difs[8])
    m1z = (difs[2] + difs[2]) + (difs[5] - difs[6]) + (difs[7] - difs[8])
    big = total(mu[i] * co(C_N + i) for i in range(19))
    ux, uy, uz = co(C_U), co(C_U + 1), co(C_U + 2)
    vx = mxx * ux + mxy * uy + mxz * uz
    vy = mxy * ux + myy * uy + myz * uz
    vz = mxz * ux + myz * uy + mzz * uz
    uv = ux * vx + uy * vy + uz * vz
    w12 = co(C_W12)
    jx = w12 * (m1x + 3.0 * vx - ux * m0) - big * co(C_G) - co(C_KX) * m1x
    jy = w12 * (m1y + 3.0 * vy - uy * m0) - big * co(C_G + 1)
    jz = w12 * (m1z + 3.0 * vz - uz * m0) - big * co(C_G + 2)
    r = co(C_UU) * m0 - co(C_W8) * uv + co(C_KXU) * m1x - big * co(C_RM)
    omb = co(C_OMB)
    odd = (jx, jy, jz, jx + jy, jx - jy, jx + jz, jx - jz, jy + jz, jy - jz)
    lam = [omb * mu[0] + r]
    for p in range(9):
        even = r + big * co(C_Q + p)
        lam.append(omb * mu[2 * p + 1] + (even + odd[p]))
        lam.append(omb * mu[2 * p + 2] + (even - odd[p]))
    return lam, m1x


def kernel(
    dims,
    thrust_ref,
    pops_hbm,
    scale_hbm,
    seed_hbm,
    map_hbm,
    out_ref,
    grad_ref,
    pops,
    scale,
    tmap,
    lam,
    halo_y,
    coef,
    gm,
    gmy,
    acc,
    push,
    rows,
    kfield,
    red,
    in_sem,
    send_sem,
    recv_sem,
    gsend_sem,
    grecv_sem,
    rsend_sem,
    rrecv_sem,
):
    n_gx, n_gy = dims
    y_hi = n_gx // (Z_CHIPS * CORES)
    x_chips = n_gy // Y_LO
    gx = lax.axis_index("gx")
    gy = lax.axis_index("gy")
    steps = 3

    loads = [pltpu.make_async_copy(map_hbm, tmap, in_sem.at[0])]
    loads.append(pltpu.make_async_copy(scale_hbm, scale, in_sem.at[1]))
    for t in (2, 1, 0):
        loads.append(pltpu.make_async_copy(pops_hbm.at[t], pops.at[t], in_sem.at[2 + t]))
    for position, member in enumerate(SLOTS):
        loads.append(
            pltpu.make_async_copy(
                seed_hbm.at[member], lam.at[0, position, pl.ds(1, 4)], in_sem.at[5 + position]
            )
        )
    for copy in loads:
        copy.start()

    right, left = lax.rem(gx + 1, n_gx), lax.rem(gx + n_gx - 1, n_gx)
    up, down = lax.rem(gy + 1, n_gy), lax.rem(gy + n_gy - 1, n_gy)
    around = (
        (left, gy),
        (right, gy),
        (gx, down),
        (gx, up),
        (left, down),
        (right, up),
        (left, up),
        (right, down),
    )
    core = lax.rem(gx, CORES)
    z = lax.rem(gx // CORES, Z_CHIPS)
    yh = gx // (CORES * Z_CHIPS)
    yl = lax.rem(gy, Y_LO)
    xc = gy // Y_LO

    def z_peer(d):
        other = lax.rem(z + d, Z_CHIPS)
        return other, ((yh * Z_CHIPS + other) * CORES + core, gy)

    def y_peer(d):
        other = lax.rem(yh * Y_LO + yl + d, y_hi * Y_LO)
        return other, (
            ((other // Y_LO) * Z_CHIPS + z) * CORES + core,
            xc * Y_LO + lax.rem(other, Y_LO),
        )

    def x_peer(d):
        other = lax.rem(xc * CORES + core + d, x_chips * CORES)
        return other, (
            (yh * Z_CHIPS + z) * CORES + lax.rem(other, CORES),
            (other // CORES) * Y_LO + yl,
        )

    phases = (
        (z_peer, z, Z_CHIPS),
        (y_peer, yh * Y_LO + yl, y_hi * Y_LO),
        (x_peer, xc * CORES + core, x_chips * CORES),
    )

    barrier = pltpu.get_barrier_semaphore()
    count = 0
    for device in around:
        pl.semaphore_signal(barrier, inc=1, device_id=device, device_id_type=MESH)
        count += 1
    for peer, _, size in phases:
        for d in range(1, size):
            pl.semaphore_signal(barrier, inc=1, device_id=peer(d)[1], device_id_type=MESH)
            count += 1

    shape = (8, 128)
    row = lax.broadcasted_iota(jnp.int32, shape, 0)
    lane = lax.broadcasted_iota(jnp.int32, shape, 1)
    row_one = lax.broadcasted_iota(jnp.int32, (1, 128), 1)

    loads[0].wait()

    turbines = thrust_ref.shape[0]

    def fill(x, _):
        ids = tmap[x]
        value = jnp.zeros(shape, F32)
        for m in range(turbines):
            value = jnp.where(ids == m, thrust_ref[m], value)
        side = 1.0 + jnp.sqrt(1.0 - value)
        kfield[x] = 4.0 * value / (side * side)
        gm[1, x + 1] = ids.astype(F32)
        acc[x] = jnp.zeros(shape, F32)
        return 0

    lax.fori_loop(0, 4, fill, 0)
    loads[1].wait()
    for t in (2, 1, 0):
        loads[2 + (2 - t)].wait()

    def prepare(i, _):
        t = i // 4
        x = lax.rem(i, 4)
        values = coefficients(
            [pops[t, member, x].astype(F32) for member in range(19)], scale[t, x], kfield[x]
        )
        for j, value in enumerate(values):
            coef[t, x, j] = value
        return 0

    lax.fori_loop(0, 12, prepare, 0)
    for x in range(4):
        gm[0, x + 1] = coef[0, x, C_GK]
    for copy in loads[5:]:
        copy.wait()
    pl.semaphore_wait(barrier, count)

    def halo_copies(e):
        parts = (
            (lam.at[e, 0:5, 1], lam.at[e, 0:5, 5]),
            (lam.at[e, 8:13, 4], lam.at[e, 8:13, 0]),
            (lam.at[e, 4:9, 1:5, 0:1], halo_y.at[e, 0, :, 1:5]),
            (lam.at[e, 12:17, 1:5, 7:8], halo_y.at[e, 1, :, 1:5]),
            (lam.at[e, 4, 1, 0:1], halo_y.at[e, 0, 0, 5]),
            (lam.at[e, 12, 4, 7:8], halo_y.at[e, 1, 0, 0]),
            (lam.at[e, 0, 1, 7:8], halo_y.at[e, 1, 4, 5]),
            (lam.at[e, 8, 4, 0:1], halo_y.at[e, 0, 4, 0]),
        )
        return [
            pltpu.make_async_remote_copy(
                src_ref=src,
                dst_ref=dst,
                send_sem=send_sem.at[e * 8 + i],
                recv_sem=recv_sem.at[e * 8 + i],
                device_id=around[i],
                device_id_type=MESH,
            )
            for i, (src, dst) in enumerate(parts)
        ]

    def field_copies():
        parts = (
            (gm.at[:, 1], gm.at[:, 5]),
            (gm.at[:, 4], gm.at[:, 0]),
            (gm.at[:, 1:5, 0:1], gmy.at[0, :, 1:5]),
            (gm.at[:, 1:5, 7:8], gmy.at[1, :, 1:5]),
            (gm.at[:, 1, 0:1], gmy.at[0, :, 5]),
            (gm.at[:, 4, 7:8], gmy.at[1, :, 0]),
            (gm.at[:, 1, 7:8], gmy.at[1, :, 5]),
            (gm.at[:, 4, 0:1], gmy.at[0, :, 0]),
        )
        return [
            pltpu.make_async_remote_copy(
                src_ref=src,
                dst_ref=dst,
                send_sem=gsend_sem.at[i],
                recv_sem=grecv_sem.at[i],
                device_id=around[i],
                device_id_type=MESH,
            )
            for i, (src, dst) in enumerate(parts)
        ]

    far_first = (4, 5, 6, 7, 0, 1, 2, 3)
    exchanges = [halo_copies(e) for e in range(steps)]
    fields = field_copies()
    for i in far_first:
        exchanges[0][i].start()
    for i in far_first:
        fields[i].start()

    def streamed(e, x):
        mu = []
        for member in range(19):
            cx, cy, cz = VELOCITIES[member]
            value = lam[e, SLOT[member], x + cx]
            if cy != 0:
                value = pltpu.roll(value, 7 if cy == 1 else 1, 0)
                side, group = (0, YP) if cy == 1 else (1, YM)
                edge = halo_y[e, side, group.index(member), x + cx]
                value = jnp.where(row == (7 if cy == 1 else 0), jnp.broadcast_to(edge, shape), value)
            if cz != 0:
                value = pltpu.roll(value, 127 if cz == 1 else 1, 1)
                value = jnp.where(
                    lane == (127 if cz == 1 else 0), lam[e, SLOT[OPPOSITE[member]], x], value
                )
            mu.append(value)
        return mu

    def plane(e, x):
        t = 2 - e
        result, m1x = transposed(streamed(e, x), lambda j: coef[t, x - 1, j])
        if e < 2:
            for position, member in enumerate(SLOTS):
                lam[e + 1, position, x] = result[member]
            acc[x - 1] += m1x * coef[t, x - 1, C_GK]
        else:
            for member in range(19):
                out_ref[member, x - 1] = result[member]
        return result

    def push_plane(x, value):
        zero = jnp.zeros(shape, F32)
        top, bottom = lane == 127, lane == 0
        first, last = row == 0, row == 7

        def lower(v):
            return jnp.where(top, zero, pltpu.roll(v, 127, 1))

        def raise_(v):
            return jnp.where(bottom, zero, pltpu.roll(v, 1, 1))

        push[0, x] = (
            (value[1] + value[1])
            + lower(value[11])
            + raise_(value[13])
            + jnp.where(last, zero, pltpu.roll(value[7], 7, 0))
            + jnp.where(first, zero, pltpu.roll(value[9], 1, 0))
        )
        push[1, x] = -(
            (value[2] + value[2])
            + raise_(value[12])
            + lower(value[14])
            + jnp.where(first, zero, pltpu.roll(value[8], 1, 0))
            + jnp.where(last, zero, pltpu.roll(value[10], 7, 0))
        )
        push[2, x] = jnp.where(top, value[12] - value[13], zero) + jnp.where(
            bottom, value[14] - value[11], zero
        )
        rows[0, 0, pl.ds(x - 1, 1), :] = value[7][0:1]
        rows[0, 1, pl.ds(x + 1, 1), :] = value[10][0:1]
        rows[1, 0, pl.ds(x - 1, 1), :] = value[9][7:8]
        rows[1, 1, pl.ds(x + 1, 1), :] = value[8][7:8]

    rows[...] = jnp.zeros((2, 2, 8, 128), F32)

    def step(e):
        for i in (2, 3):
            exchanges[e][i].wait_recv()

        def inner(i, _):
            result = plane(e, 2 + i)
            if e == 1:
                push_plane(2 + i, result)
            return 0

        lax.fori_loop(0, 2, inner, 0)
        for i in (0, 1, 4, 5, 6, 7):
            exchanges[e][i].wait_recv()

        def outer(i, _):
            result = plane(e, 1 + 3 * i)
            if e == 1:
                push_plane(1 + 3 * i, result)
            return 0

        lax.fori_loop(0, 2, outer, 0)
        if e < 2:
            for i in far_first:
                exchanges[e + 1][i].start()

    step(0)
    step(1)

    for copy in fields:
        copy.wait_recv()
    zero = jnp.zeros(shape, F32)
    weights, ids = [], []
    for x in range(6):
        value = zero
        if x + 1 <= 4:
            value = value + push[0, x + 1]
        if x - 1 >= 1:
            value = value + push[1, x - 1]
        if 1 <= x <= 4:
            value = (value + push[2, x]) * gm[0, x] + acc[x - 1]
        else:
            value = value * gm[0, x]
        weights.append(value)
        ids.append(gm[1, x])
    for side in range(2):
        value = rows[side, 0] - rows[side, 1]
        g = jnp.concatenate([gmy[1 - side, 0, x] for x in range(6)] + [jnp.zeros((2, 128), F32)], 0)
        m = jnp.concatenate([gmy[1 - side, 1, x] for x in range(6)] + [jnp.full((2, 128), -1.0, F32)], 0)
        weights.append(value * g)
        ids.append(m)
    collected = zero
    for m in range(turbines):
        part = total(jnp.where(ids[i] == float(m), weights[i], zero) for i in range(8))
        collected = jnp.where(lane == m, jnp.sum(part, axis=1, keepdims=True), collected)
    partial = jnp.sum(collected, axis=0, keepdims=True)

    reduced = []
    copies = []
    for phase, (peer, mine, size) in enumerate(phases):
        red[phase, mine] = partial
        started = []
        for d in range(1, size):
            _, device = peer(d)
            started.append(
                pltpu.make_async_remote_copy(
                    src_ref=red.at[phase, mine],
                    dst_ref=red.at[phase, mine],
                    send_sem=rsend_sem.at[phase, d],
                    recv_sem=rrecv_sem.at[phase, d],
                    device_id=device,
                    device_id_type=MESH,
                )
            )
        for copy in started:
            copy.start()
        copies += started
        if phase == 0:
            step(2)
        for copy in started:
            copy.wait_recv()
        partial = total(red[phase, j] for j in range(size))

    thrust = jnp.zeros((1, 128), F32)
    for m in range(turbines):
        thrust = jnp.where(row_one == m, thrust_ref[m], thrust)
    side = jnp.sqrt(1.0 - thrust)
    slope = 4.0 / (side * ((1.0 + side) * (1.0 + side)))
    grad_ref[...] = (partial * slope)[0, 0:turbines]

    for group in exchanges + [fields, copies]:
        for copy in group:
            copy.wait_send()


def shards(n_gx, n_gy, fwd_pops, fwd_scale, seed_adjoint, turbine_map, thrust):
    phase_max = max(Z_CHIPS, n_gx // (Z_CHIPS * CORES) * Y_LO, n_gy // Y_LO * CORES)
    hbm = pl.BlockSpec(memory_space=pl.ANY)
    vmem = pl.BlockSpec(memory_space=pltpu.VMEM)
    return pl.pallas_call(
        functools.partial(kernel, (n_gx, n_gy)),
        out_shape=(
            jax.ShapeDtypeStruct(seed_adjoint.shape, F32),
            jax.ShapeDtypeStruct(thrust.shape, F32),
        ),
        in_specs=[pl.BlockSpec(memory_space=pltpu.SMEM), hbm, hbm, hbm, hbm],
        out_specs=(vmem, vmem),
        scratch_shapes=[
            pltpu.VMEM(fwd_pops.shape, fwd_pops.dtype),
            pltpu.VMEM(fwd_scale.shape, F32),
            pltpu.VMEM(turbine_map.shape, jnp.int32),
            pltpu.VMEM((3, 20, 6, 8, 128), F32),
            pltpu.VMEM((3, 2, 5, 6, 1, 128), F32),
            pltpu.VMEM((3, 4, N_COEF, 8, 128), F32),
            pltpu.VMEM((2, 6, 8, 128), F32),
            pltpu.VMEM((2, 2, 6, 1, 128), F32),
            pltpu.VMEM((4, 8, 128), F32),
            pltpu.VMEM((3, 5, 8, 128), F32),
            pltpu.VMEM((2, 2, 8, 128), F32),
            pltpu.VMEM((4, 8, 128), F32),
            pltpu.VMEM((3, phase_max, 1, 128), F32),
            pltpu.SemaphoreType.DMA((25,)),
            pltpu.SemaphoreType.DMA((24,)),
            pltpu.SemaphoreType.DMA((24,)),
            pltpu.SemaphoreType.DMA((8,)),
            pltpu.SemaphoreType.DMA((8,)),
            pltpu.SemaphoreType.DMA((3, phase_max)),
            pltpu.SemaphoreType.DMA((3, phase_max)),
        ],
        compiler_params=pltpu.CompilerParams(collective_id=0, has_side_effects=True),
        name="adjoint",
    )(thrust, fwd_pops, fwd_scale, seed_adjoint, turbine_map)


def solution(mesh):
    placed = (
        P(None, None, "gx", "gy", None),
        P(None, "gx", "gy", None),
        P(None, "gx", "gy", None),
        P("gx", "gy", None),
        P(),
    )
    return jax.shard_map(
        functools.partial(shards, mesh.shape["gx"], mesh.shape["gy"]),
        mesh=mesh,
        in_specs=placed,
        out_specs=(P(None, "gx", "gy", None), P()),
        check_vma=False,
    )
```

```python
import functools

import jax
import jax.numpy as jnp
from jax import lax
from jax.experimental import pallas as pl
from jax.experimental.pallas import tpu as pltpu
from jax.sharding import PartitionSpec as P

MESH = pl.DeviceIdType.MESH
F32 = jnp.float32

VELOCITIES = (
    (0, 0, 0),
    (1, 0, 0),
    (-1, 0, 0),
    (0, 1, 0),
    (0, -1, 0),
    (0, 0, 1),
    (0, 0, -1),
    (1, 1, 0),
    (-1, -1, 0),
    (1, -1, 0),
    (-1, 1, 0),
    (1, 0, 1),
    (-1, 0, -1),
    (1, 0, -1),
    (-1, 0, 1),
    (0, 1, 1),
    (0, -1, -1),
    (0, 1, -1),
    (0, -1, 1),
)
OPPOSITE = (0, 2, 1, 4, 3, 6, 5, 8, 7, 10, 9, 12, 11, 14, 13, 16, 15, 18, 17)
WEIGHTS = tuple([1.0 / 3.0] + [1.0 / 18.0] * 6 + [1.0 / 36.0] * 12)
MEAN_FLOW = 0.1
TAU_BASE = 0.51
SMAG_COEF = 18.0 * 1.4142135623730951 * 0.17 * 0.17
QUAD_FLOOR = 0.0001

SLOTS = (9, 1, 11, 13, 7, 3, 15, 17, 10, 2, 12, 14, 8, 4, 16, 18, 9, 0, 5, 6)
SLOT = {member: SLOTS.index(member) for member in range(19)}
YP = SLOTS[4:9]
YM = SLOTS[12:17]
CORES = 2
Z_CHIPS = 8
Y_LO = 2

C_N = 0
C_Q = 19
C_G = 28
C_U = 31
C_RM, C_OMB, C_W12, C_UU, C_W8, C_KX, C_KXU, C_GK = range(34, 42)
N_COEF = 42


def base_values():
    values = []
    for member in range(19):
        along = float(VELOCITIES[member][0])
        values.append(
            WEIGHTS[member]
            * (
                1.0
                + 3.0 * MEAN_FLOW * along
                + 4.5 * MEAN_FLOW * MEAN_FLOW * along * along
                - 1.5 * MEAN_FLOW * MEAN_FLOW
            )
        )
    return values


def total(terms):
    terms = list(terms)
    while len(terms) > 1:
        terms = [
            terms[i] + terms[i + 1] if i + 1 < len(terms) else terms[i]
            for i in range(0, len(terms), 2)
        ]
    return terms[0]


def second_moments(pair):
    sx, sy, sz, a, b, c, d, e, f = pair
    txy, txz, tyz = a + b, c + d, e + f
    return sx, sy, sz, txy, txz, tyz, a - b, c - d, e - f


def coefficients(pops, scale, k):
    base = base_values()
    f = [base[i] + (base[i] * scale) * pops[i] for i in range(19)]
    rho = total(f)
    sums = [f[2 * p + 1] + f[2 * p + 2] for p in range(9)]
    difs = [f[2 * p + 1] - f[2 * p + 2] for p in range(9)]
    jx = (difs[0] + difs[3] + difs[4]) + (difs[5] + difs[6])
    jy = (difs[1] + difs[3] - difs[4]) + (difs[7] + difs[8])
    jz = (difs[2] + difs[5] - difs[6]) + (difs[7] - difs[8])
    inv = 1.0 / rho
    u = (jx * inv, jy * inv, jz * inv)
    u2 = u[0] * u[0] + u[1] * u[1] + u[2] * u[2]
    rest = 1.0 - 1.5 * u2
    n = [None] * 19
    third = rho * (1.0 / 3.0)
    n[0] = f[0] - third * rest
    r18 = rho * (1.0 / 18.0)
    r36 = rho * (1.0 / 36.0)
    proj = (
        u[0],
        u[1],
        u[2],
        u[0] + u[1],
        u[0] - u[1],
        u[0] + u[2],
        u[0] - u[2],
        u[1] + u[2],
        u[1] - u[2],
    )
    for p in range(9):
        even = rest + 4.5 * (proj[p] * proj[p])
        odd = 3.0 * proj[p]
        weight = r18 if p < 3 else r36
        n[2 * p + 1] = f[2 * p + 1] - weight * (even + odd)
        n[2 * p + 2] = f[2 * p + 2] - weight * (even - odd)
    pair = [n[2 * p + 1] + n[2 * p + 2] for p in range(9)]
    sx, sy, sz, txy, txz, tyz, pxy, pxz, pyz = second_moments(pair)
    pxx = sx + txy + txz
    pyy = sy + txy + tyz
    pzz = sz + txz + tyz
    square = (pxx * pxx + pyy * pyy + pzz * pzz) + 2.0 * (
        pxy * pxy + pxz * pxz + pyz * pyz
    )
    q = jnp.sqrt(square + QUAD_FLOOR)
    s = jnp.sqrt(TAU_BASE * TAU_BASE + SMAG_COEF * (q * inv))
    om = 2.0 / (TAU_BASE + s)
    a1 = (om * om) * (0.25 * SMAG_COEF) * inv / (s * q)
    a2 = a1 * (q * q) * inv
    pu = (
        pxx * u[0] + pxy * u[1] + pxz * u[2],
        pxy * u[0] + pyy * u[1] + pyz * u[2],
        pxz * u[0] + pyz * u[1] + pzz * u[2],
    )
    upu = u[0] * pu[0] + u[1] * pu[1] + u[2] * pu[2]
    trace = pxx + pyy + pzz
    quads = (
        pxx,
        pyy,
        pzz,
        pxx + pyy + 2.0 * pxy,
        pxx + pyy - 2.0 * pxy,
        pxx + pzz + 2.0 * pxz,
        pxx + pzz - 2.0 * pxz,
        pyy + pzz + 2.0 * pyz,
        pyy + pzz - 2.0 * pyz,
    )
    absu = jnp.abs(u[0])
    kx = k * absu * inv * (1.0 / 12.0)
    out = list(n)
    out += [a1 * value for value in quads]
    out += [(2.0 * a1) * value for value in pu]
    out += list(u)
    out += [
        a2 + a1 * (trace * (1.0 / 3.0) - upu),
        1.0 - om,
        om * (1.0 / 12.0),
        om * (1.0 / 36.0) * (1.0 + 1.5 * u2),
        om * 0.125,
        kx,
        kx * u[0],
        (-1.5 / 36.0) * (u[0] * absu),
    ]
    return out


def transposed(mu, co):
    sums = [mu[2 * p + 1] + mu[2 * p + 2] for p in range(9)]
    difs = [mu[2 * p + 1] - mu[2 * p + 2] for p in range(9)]
    sx, sy, sz, txy, txz, tyz, mxy, mxz, myz = second_moments(sums)
    sx, sy, sz = sx + sx, sy + sy, sz + sz
    mxx = sx + txy + txz
    myy = sy + txy + tyz
    mzz = sz + txz + tyz
    m0 = 12.0 * mu[0] + ((sx + sy + sz) + (txy + txz + tyz))
    m1x = (difs[0] + difs[0]) + (difs[3] + difs[4]) + (difs[5] + difs[6])
    m1y = (difs[1] + difs[1]) + (difs[3] - difs[4]) + (difs[7] + difs[8])
    m1z = (difs[2] + difs[2]) + (difs[5] - difs[6]) + (difs[7] - difs[8])
    big = total(mu[i] * co(C_N + i) for i in range(19))
    ux, uy, uz = co(C_U), co(C_U + 1), co(C_U + 2)
    vx = mxx * ux + mxy * uy + mxz * uz
    vy = mxy * ux + myy * uy + myz * uz
    vz = mxz * ux + myz * uy + mzz * uz
    uv = ux * vx + uy * vy + uz * vz
    w12 = co(C_W12)
    jx = w12 * (m1x + 3.0 * vx - ux * m0) - big * co(C_G) - co(C_KX) * m1x
    jy = w12 * (m1y + 3.0 * vy - uy * m0) - big * co(C_G + 1)
    jz = w12 * (m1z + 3.0 * vz - uz * m0) - big * co(C_G + 2)
    r = co(C_UU) * m0 - co(C_W8) * uv + co(C_KXU) * m1x - big * co(C_RM)
    omb = co(C_OMB)
    odd = (jx, jy, jz, jx + jy, jx - jy, jx + jz, jx - jz, jy + jz, jy - jz)
    lam = [omb * mu[0] + r]
    for p in range(9):
        even = r + big * co(C_Q + p)
        lam.append(omb * mu[2 * p + 1] + (even + odd[p]))
        lam.append(omb * mu[2 * p + 2] + (even - odd[p]))
    return lam, m1x


def kernel(
    dims,
    thrust_hbm,
    pops_hbm,
    scale_hbm,
    seed_hbm,
    map_hbm,
    out_ref,
    grad_ref,
    pops,
    scale,
    thrust_ref,
    tmap,
    lam,
    halo_y,
    coef,
    gm,
    gmy,
    acc,
    push,
    rows,
    kfield,
    red,
    in_sem,
    send_sem,
    recv_sem,
    gsend_sem,
    grecv_sem,
    rsend_sem,
    rrecv_sem,
):
    n_gx, n_gy = dims
    y_hi = n_gx // (Z_CHIPS * CORES)
    x_chips = n_gy // Y_LO
    gx = lax.axis_index("gx")
    gy = lax.axis_index("gy")
    steps = 3

    right, left = lax.rem(gx + 1, n_gx), lax.rem(gx + n_gx - 1, n_gx)
    up, down = lax.rem(gy + 1, n_gy), lax.rem(gy + n_gy - 1, n_gy)
    around = (
        (left, gy),
        (right, gy),
        (gx, down),
        (gx, up),
        (left, down),
        (right, up),
        (left, up),
        (right, down),
    )
    core = lax.rem(gx, CORES)
    z = lax.rem(gx // CORES, Z_CHIPS)
    yh = gx // (CORES * Z_CHIPS)
    yl = lax.rem(gy, Y_LO)
    xc = gy // Y_LO

    def z_peer(d):
        other = lax.rem(z + d, Z_CHIPS)
        return other, ((yh * Z_CHIPS + other) * CORES + core, gy)

    def y_peer(d):
        other = lax.rem(yh * Y_LO + yl + d, y_hi * Y_LO)
        return other, (
            ((other // Y_LO) * Z_CHIPS + z) * CORES + core,
            xc * Y_LO + lax.rem(other, Y_LO),
        )

    def x_peer(d):
        other = lax.rem(xc * CORES + core + d, x_chips * CORES)
        return other, (
            (yh * Z_CHIPS + z) * CORES + lax.rem(other, CORES),
            (other // CORES) * Y_LO + yl,
        )

    phases = (
        (x_peer, xc * CORES + core, x_chips * CORES),
        (z_peer, z, Z_CHIPS),
        (y_peer, yh * Y_LO + yl, y_hi * Y_LO),
    )

    barrier = pltpu.get_barrier_semaphore()
    count = 0
    far_first = (4, 5, 6, 7, 0, 1, 2, 3)
    for i in far_first:
        pl.semaphore_signal(barrier, inc=1, device_id=around[i], device_id_type=MESH)
        count += 1

    loads = [pltpu.make_async_copy(map_hbm, tmap, in_sem.at[0])]
    loads.append(pltpu.make_async_copy(scale_hbm, scale, in_sem.at[1]))
    for t in (2, 1, 0):
        loads.append(pltpu.make_async_copy(pops_hbm.at[t], pops.at[t], in_sem.at[2 + t]))
    for position, member in enumerate(SLOTS):
        loads.append(
            pltpu.make_async_copy(
                seed_hbm.at[member], lam.at[0, position, pl.ds(1, 4)], in_sem.at[5 + position]
            )
        )
    loads.append(pltpu.make_async_copy(thrust_hbm, thrust_ref, in_sem.at[25]))
    for copy in loads:
        copy.start()

    for peer, _, size in phases:
        for d in range(1, size):
            pl.semaphore_signal(barrier, inc=1, device_id=peer(d)[1], device_id_type=MESH)
            count += 1

    shape = (8, 128)
    row = lax.broadcasted_iota(jnp.int32, shape, 0)
    lane = lax.broadcasted_iota(jnp.int32, shape, 1)
    row_one = lax.broadcasted_iota(jnp.int32, (1, 128), 1)

    loads[0].wait()
    loads[-1].wait()

    turbines = thrust_ref.shape[0]

    def fill(x, _):
        ids = tmap[x]
        value = jnp.zeros(shape, F32)
        for m in range(turbines):
            value = jnp.where(ids == m, thrust_ref[m], value)
        side = 1.0 + jnp.sqrt(1.0 - value)
        kfield[x] = 4.0 * value / (side * side)
        gm[1, x + 1] = ids.astype(F32)
        acc[x] = jnp.zeros(shape, F32)
        return 0

    lax.fori_loop(0, 4, fill, 0)
    loads[1].wait()
    for t in (2, 1, 0):
        loads[2 + (2 - t)].wait()

    def prepare(i, _):
        t = i // 4
        x = lax.rem(i, 4)
        values = coefficients(
            [pops[t, member, x].astype(F32) for member in range(19)], scale[t, x], kfield[x]
        )
        for j, value in enumerate(values):
            coef[t, x, j] = value
        return 0

    lax.fori_loop(0, 12, prepare, 0)
    for x in range(4):
        gm[0, x + 1] = coef[0, x, C_GK]
    for copy in loads[5:-1]:
        copy.wait()
    pl.semaphore_wait(barrier, count)

    def halo_copies(e):
        parts = (
            (lam.at[e, 0:5, 1], lam.at[e, 0:5, 5]),
            (lam.at[e, 8:13, 4], lam.at[e, 8:13, 0]),
            (lam.at[e, 4:9, 1:5, 0:1], halo_y.at[e, 0, :, 1:5]),
            (lam.at[e, 12:17, 1:5, 7:8], halo_y.at[e, 1, :, 1:5]),
            (lam.at[e, 4, 1, 0:1], halo_y.at[e, 0, 0, 5]),
            (lam.at[e, 12, 4, 7:8], halo_y.at[e, 1, 0, 0]),
            (lam.at[e, 0, 1, 7:8], halo_y.at[e, 1, 4, 5]),
            (lam.at[e, 8, 4, 0:1], halo_y.at[e, 0, 4, 0]),
        )
        return [
            pltpu.make_async_remote_copy(
                src_ref=src,
                dst_ref=dst,
                send_sem=send_sem.at[e * 8 + i],
                recv_sem=recv_sem.at[e * 8 + i],
                device_id=around[i],
                device_id_type=MESH,
            )
            for i, (src, dst) in enumerate(parts)
        ]

    def field_copies():
        parts = (
            (gm.at[:, 1], gm.at[:, 5]),
            (gm.at[:, 4], gm.at[:, 0]),
            (gm.at[:, 1:5, 0:1], gmy.at[0, :, 1:5]),
            (gm.at[:, 1:5, 7:8], gmy.at[1, :, 1:5]),
            (gm.at[:, 1, 0:1], gmy.at[0, :, 5]),
            (gm.at[:, 4, 7:8], gmy.at[1, :, 0]),
            (gm.at[:, 1, 7:8], gmy.at[1, :, 5]),
            (gm.at[:, 4, 0:1], gmy.at[0, :, 0]),
        )
        return [
            pltpu.make_async_remote_copy(
                src_ref=src,
                dst_ref=dst,
                send_sem=gsend_sem.at[i],
                recv_sem=grecv_sem.at[i],
                device_id=around[i],
                device_id_type=MESH,
            )
            for i, (src, dst) in enumerate(parts)
        ]

    exchanges = [halo_copies(e) for e in range(steps)]
    fields = field_copies()
    for i in far_first:
        exchanges[0][i].start()
    for i in far_first:
        fields[i].start()

    def streamed(e, x):
        mu = []
        for member in range(19):
            cx, cy, cz = VELOCITIES[member]
            value = lam[e, SLOT[member], x + cx]
            if cy != 0:
                value = pltpu.roll(value, 7 if cy == 1 else 1, 0)
                side, group = (0, YP) if cy == 1 else (1, YM)
                edge = halo_y[e, side, group.index(member), x + cx]
                value = jnp.where(row == (7 if cy == 1 else 0), jnp.broadcast_to(edge, shape), value)
            if cz != 0:
                value = pltpu.roll(value, 127 if cz == 1 else 1, 1)
                value = jnp.where(
                    lane == (127 if cz == 1 else 0), lam[e, SLOT[OPPOSITE[member]], x], value
                )
            mu.append(value)
        return mu

    def plane(e, x):
        t = 2 - e
        result, m1x = transposed(streamed(e, x), lambda j: coef[t, x - 1, j])
        if e < 2:
            for position, member in enumerate(SLOTS):
                lam[e + 1, position, x] = result[member]
            acc[x - 1] += m1x * coef[t, x - 1, C_GK]
        else:
            for member in range(19):
                out_ref[member, x - 1] = result[member]
        return result

    def push_plane(x, value):
        zero = jnp.zeros(shape, F32)
        top, bottom = lane == 127, lane == 0
        first, last = row == 0, row == 7

        def lower(v):
            return jnp.where(top, zero, pltpu.roll(v, 127, 1))

        def raise_(v):
            return jnp.where(bottom, zero, pltpu.roll(v, 1, 1))

        push[0, x] = (
            (value[1] + value[1])
            + lower(value[11])
            + raise_(value[13])
            + jnp.where(last, zero, pltpu.roll(value[7], 7, 0))
            + jnp.where(first, zero, pltpu.roll(value[9], 1, 0))
        )
        push[1, x] = -(
            (value[2] + value[2])
            + raise_(value[12])
            + lower(value[14])
            + jnp.where(first, zero, pltpu.roll(value[8], 1, 0))
            + jnp.where(last, zero, pltpu.roll(value[10], 7, 0))
        )
        push[2, x] = jnp.where(top, value[12] - value[13], zero) + jnp.where(
            bottom, value[14] - value[11], zero
        )
        rows[0, 0, pl.ds(x - 1, 1), :] = value[7][0:1]
        rows[0, 1, pl.ds(x + 1, 1), :] = value[10][0:1]
        rows[1, 0, pl.ds(x - 1, 1), :] = value[9][7:8]
        rows[1, 1, pl.ds(x + 1, 1), :] = value[8][7:8]

    rows[...] = jnp.zeros((2, 2, 8, 128), F32)

    def step(e):
        for i in (2, 3):
            exchanges[e][i].wait_recv()

        def inner(i, _):
            result = plane(e, 2 + i)
            if e == 1:
                push_plane(2 + i, result)
            return 0

        lax.fori_loop(0, 2, inner, 0)
        for i in (0, 1, 4, 5, 6, 7):
            exchanges[e][i].wait_recv()

        def outer(i, _):
            result = plane(e, 1 + 3 * i)
            if e == 1:
                push_plane(1 + 3 * i, result)
            return 0

        lax.fori_loop(0, 2, outer, 0)
        if e < 2:
            for i in far_first:
                exchanges[e + 1][i].start()

    step(0)
    step(1)

    for copy in fields:
        copy.wait_recv()
    zero = jnp.zeros(shape, F32)
    weights, ids = [], []
    for x in range(6):
        value = zero
        if x + 1 <= 4:
            value = value + push[0, x + 1]
        if x - 1 >= 1:
            value = value + push[1, x - 1]
        if 1 <= x <= 4:
            value = (value + push[2, x]) * gm[0, x] + acc[x - 1]
        else:
            value = value * gm[0, x]
        weights.append(value)
        ids.append(gm[1, x])
    for side in range(2):
        value = rows[side, 0] - rows[side, 1]
        g = jnp.concatenate([gmy[1 - side, 0, x] for x in range(6)] + [jnp.zeros((2, 128), F32)], 0)
        m = jnp.concatenate([gmy[1 - side, 1, x] for x in range(6)] + [jnp.full((2, 128), -1.0, F32)], 0)
        weights.append(value * g)
        ids.append(m)
    collected = zero
    for m in range(turbines):
        part = total(jnp.where(ids[i] == float(m), weights[i], zero) for i in range(8))
        collected = jnp.where(lane == m, jnp.sum(part, axis=1, keepdims=True), collected)
    partial = jnp.sum(collected, axis=0, keepdims=True)

    reduced = []
    copies = []
    for phase, (peer, mine, size) in enumerate(phases):
        red[phase, mine] = partial
        started = []
        for d in range(1, size):
            _, device = peer(d)
            started.append(
                pltpu.make_async_remote_copy(
                    src_ref=red.at[phase, mine],
                    dst_ref=red.at[phase, mine],
                    send_sem=rsend_sem.at[phase, d],
                    recv_sem=rrecv_sem.at[phase, d],
                    device_id=device,
                    device_id_type=MESH,
                )
            )
        for copy in started:
            copy.start()
        copies += started
        if phase == len(phases) - 1:
            step(2)
        for copy in started:
            copy.wait_recv()
        partial = total(red[phase, j] for j in range(size))

    thrust = jnp.zeros((1, 128), F32)
    for m in range(turbines):
        thrust = jnp.where(row_one == m, thrust_ref[m], thrust)
    side = jnp.sqrt(1.0 - thrust)
    slope = 4.0 / (side * ((1.0 + side) * (1.0 + side)))
    grad_ref[...] = (partial * slope)[0, 0:turbines]

    for group in exchanges + [fields, copies]:
        for copy in group:
            copy.wait_send()


def write_kernel(adjoint_vmem, grad_vmem, adjoint_out, grad_out, sem):
    copies = (
        pltpu.make_async_copy(adjoint_vmem, adjoint_out, sem.at[0]),
        pltpu.make_async_copy(grad_vmem, grad_out, sem.at[1]),
    )
    for copy in copies:
        copy.start()
    for copy in copies:
        copy.wait()


def shards(n_gx, n_gy, fwd_pops, fwd_scale, seed_adjoint, turbine_map, thrust):
    phase_max = max(Z_CHIPS, n_gx // (Z_CHIPS * CORES) * Y_LO, n_gy // Y_LO * CORES)
    hbm = pl.BlockSpec(memory_space=pl.ANY)
    vmem = pl.BlockSpec(memory_space=pltpu.VMEM)
    results = pl.pallas_call(
        functools.partial(kernel, (n_gx, n_gy)),
        out_shape=(pltpu.VMEM(seed_adjoint.shape, F32), pltpu.VMEM(thrust.shape, F32)),
        in_specs=[hbm, hbm, hbm, hbm, hbm],
        out_specs=(vmem, vmem),
        scratch_shapes=[
            pltpu.VMEM(fwd_pops.shape, fwd_pops.dtype),
            pltpu.VMEM(fwd_scale.shape, F32),
            pltpu.SMEM(thrust.shape, F32),
            pltpu.VMEM(turbine_map.shape, jnp.int32),
            pltpu.VMEM((3, 20, 6, 8, 128), F32),
            pltpu.VMEM((3, 2, 5, 6, 1, 128), F32),
            pltpu.VMEM((3, 4, N_COEF, 8, 128), F32),
            pltpu.VMEM((2, 6, 8, 128), F32),
            pltpu.VMEM((2, 2, 6, 1, 128), F32),
            pltpu.VMEM((4, 8, 128), F32),
            pltpu.VMEM((3, 5, 8, 128), F32),
            pltpu.VMEM((2, 2, 8, 128), F32),
            pltpu.VMEM((4, 8, 128), F32),
            pltpu.VMEM((3, phase_max, 1, 128), F32),
            pltpu.SemaphoreType.DMA((26,)),
            pltpu.SemaphoreType.DMA((24,)),
            pltpu.SemaphoreType.DMA((24,)),
            pltpu.SemaphoreType.DMA((8,)),
            pltpu.SemaphoreType.DMA((8,)),
            pltpu.SemaphoreType.DMA((3, phase_max)),
            pltpu.SemaphoreType.DMA((3, phase_max)),
        ],
        compiler_params=pltpu.CompilerParams(collective_id=0, has_side_effects=True),
        name="adjoint",
    )(thrust, fwd_pops, fwd_scale, seed_adjoint, turbine_map)
    return pl.pallas_call(
        write_kernel,
        out_shape=(
            jax.ShapeDtypeStruct(seed_adjoint.shape, F32),
            jax.ShapeDtypeStruct(thrust.shape, F32),
        ),
        in_specs=[vmem, vmem],
        out_specs=(hbm, hbm),
        scratch_shapes=[pltpu.SemaphoreType.DMA((2,))],
        name="write",
    )(*[pltpu.with_memory_space_constraint(r, pltpu.VMEM) for r in results])


def solution(mesh):
    placed = (
        P(None, None, "gx", "gy", None),
        P(None, "gx", "gy", None),
        P(None, "gx", "gy", None),
        P("gx", "gy", None),
        P(),
    )
    return jax.shard_map(
        functools.partial(shards, mesh.shape["gx"], mesh.shape["gy"]),
        mesh=mesh,
        in_specs=placed,
        out_specs=(P(None, "gx", "gy", None), P()),
        check_vma=False,
    )
```

```python
import functools

import jax
import jax.numpy as jnp
from jax import lax
from jax.experimental import pallas as pl
from jax.experimental.pallas import tpu as pltpu
from jax.sharding import PartitionSpec as P

MESH = pl.DeviceIdType.MESH
F32 = jnp.float32

VELOCITIES = (
    (0, 0, 0),
    (1, 0, 0),
    (-1, 0, 0),
    (0, 1, 0),
    (0, -1, 0),
    (0, 0, 1),
    (0, 0, -1),
    (1, 1, 0),
    (-1, -1, 0),
    (1, -1, 0),
    (-1, 1, 0),
    (1, 0, 1),
    (-1, 0, -1),
    (1, 0, -1),
    (-1, 0, 1),
    (0, 1, 1),
    (0, -1, -1),
    (0, 1, -1),
    (0, -1, 1),
)
OPPOSITE = (0, 2, 1, 4, 3, 6, 5, 8, 7, 10, 9, 12, 11, 14, 13, 16, 15, 18, 17)
WEIGHTS = tuple([1.0 / 3.0] + [1.0 / 18.0] * 6 + [1.0 / 36.0] * 12)
MEAN_FLOW = 0.1
TAU_BASE = 0.51
SMAG_COEF = 18.0 * 1.4142135623730951 * 0.17 * 0.17
QUAD_FLOOR = 0.0001

SLOTS = (9, 1, 11, 13, 7, 3, 15, 17, 10, 2, 12, 14, 8, 4, 16, 18, 9, 0, 5, 6)
SLOT = {member: SLOTS.index(member) for member in range(19)}
YP = SLOTS[4:9]
YM = SLOTS[12:17]
CORES = 2
Z_CHIPS = 8
Y_LO = 2

C_N = 0
C_Q = 19
C_G = 28
C_U = 31
C_RM, C_OMB, C_W12, C_UU, C_W8, C_KX, C_KXU, C_GK = range(34, 42)
N_COEF = 42


def base_values():
    values = []
    for member in range(19):
        along = float(VELOCITIES[member][0])
        values.append(
            WEIGHTS[member]
            * (
                1.0
                + 3.0 * MEAN_FLOW * along
                + 4.5 * MEAN_FLOW * MEAN_FLOW * along * along
                - 1.5 * MEAN_FLOW * MEAN_FLOW
            )
        )
    return values


def total(terms):
    terms = list(terms)
    while len(terms) > 1:
        terms = [
            terms[i] + terms[i + 1] if i + 1 < len(terms) else terms[i]
            for i in range(0, len(terms), 2)
        ]
    return terms[0]


def second_moments(pair):
    sx, sy, sz, a, b, c, d, e, f = pair
    txy, txz, tyz = a + b, c + d, e + f
    return sx, sy, sz, txy, txz, tyz, a - b, c - d, e - f


def coefficients(pops, scale, k):
    base = base_values()
    f = [base[i] + (base[i] * scale) * pops[i] for i in range(19)]
    rho = total(f)
    sums = [f[2 * p + 1] + f[2 * p + 2] for p in range(9)]
    difs = [f[2 * p + 1] - f[2 * p + 2] for p in range(9)]
    jx = (difs[0] + difs[3] + difs[4]) + (difs[5] + difs[6])
    jy = (difs[1] + difs[3] - difs[4]) + (difs[7] + difs[8])
    jz = (difs[2] + difs[5] - difs[6]) + (difs[7] - difs[8])
    inv = 1.0 / rho
    u = (jx * inv, jy * inv, jz * inv)
    u2 = u[0] * u[0] + u[1] * u[1] + u[2] * u[2]
    rest = 1.0 - 1.5 * u2
    n = [None] * 19
    third = rho * (1.0 / 3.0)
    n[0] = f[0] - third * rest
    r18 = rho * (1.0 / 18.0)
    r36 = rho * (1.0 / 36.0)
    proj = (
        u[0],
        u[1],
        u[2],
        u[0] + u[1],
        u[0] - u[1],
        u[0] + u[2],
        u[0] - u[2],
        u[1] + u[2],
        u[1] - u[2],
    )
    for p in range(9):
        even = rest + 4.5 * (proj[p] * proj[p])
        odd = 3.0 * proj[p]
        weight = r18 if p < 3 else r36
        n[2 * p + 1] = f[2 * p + 1] - weight * (even + odd)
        n[2 * p + 2] = f[2 * p + 2] - weight * (even - odd)
    pair = [n[2 * p + 1] + n[2 * p + 2] for p in range(9)]
    sx, sy, sz, txy, txz, tyz, pxy, pxz, pyz = second_moments(pair)
    pxx = sx + txy + txz
    pyy = sy + txy + tyz
    pzz = sz + txz + tyz
    square = (pxx * pxx + pyy * pyy + pzz * pzz) + 2.0 * (
        pxy * pxy + pxz * pxz + pyz * pyz
    )
    q = jnp.sqrt(square + QUAD_FLOOR)
    s = jnp.sqrt(TAU_BASE * TAU_BASE + SMAG_COEF * (q * inv))
    om = 2.0 / (TAU_BASE + s)
    a1 = (om * om) * (0.25 * SMAG_COEF) * inv / (s * q)
    a2 = a1 * (q * q) * inv
    pu = (
        pxx * u[0] + pxy * u[1] + pxz * u[2],
        pxy * u[0] + pyy * u[1] + pyz * u[2],
        pxz * u[0] + pyz * u[1] + pzz * u[2],
    )
    upu = u[0] * pu[0] + u[1] * pu[1] + u[2] * pu[2]
    trace = pxx + pyy + pzz
    quads = (
        pxx,
        pyy,
        pzz,
        pxx + pyy + 2.0 * pxy,
        pxx + pyy - 2.0 * pxy,
        pxx + pzz + 2.0 * pxz,
        pxx + pzz - 2.0 * pxz,
        pyy + pzz + 2.0 * pyz,
        pyy + pzz - 2.0 * pyz,
    )
    absu = jnp.abs(u[0])
    kx = k * absu * inv * (1.0 / 12.0)
    out = list(n)
    out += [a1 * value for value in quads]
    out += [(2.0 * a1) * value for value in pu]
    out += list(u)
    out += [
        a2 + a1 * (trace * (1.0 / 3.0) - upu),
        1.0 - om,
        om * (1.0 / 12.0),
        om * (1.0 / 36.0) * (1.0 + 1.5 * u2),
        om * 0.125,
        kx,
        kx * u[0],
        (-1.5 / 36.0) * (u[0] * absu),
    ]
    return out


def transposed(mu, co):
    sums = [mu[2 * p + 1] + mu[2 * p + 2] for p in range(9)]
    difs = [mu[2 * p + 1] - mu[2 * p + 2] for p in range(9)]
    sx, sy, sz, txy, txz, tyz, mxy, mxz, myz = second_moments(sums)
    sx, sy, sz = sx + sx, sy + sy, sz + sz
    mxx = sx + txy + txz
    myy = sy + txy + tyz
    mzz = sz + txz + tyz
    m0 = 12.0 * mu[0] + ((sx + sy + sz) + (txy + txz + tyz))
    m1x = (difs[0] + difs[0]) + (difs[3] + difs[4]) + (difs[5] + difs[6])
    m1y = (difs[1] + difs[1]) + (difs[3] - difs[4]) + (difs[7] + difs[8])
    m1z = (difs[2] + difs[2]) + (difs[5] - difs[6]) + (difs[7] - difs[8])
    big = total(mu[i] * co(C_N + i) for i in range(19))
    ux, uy, uz = co(C_U), co(C_U + 1), co(C_U + 2)
    vx = mxx * ux + mxy * uy + mxz * uz
    vy = mxy * ux + myy * uy + myz * uz
    vz = mxz * ux + myz * uy + mzz * uz
    uv = ux * vx + uy * vy + uz * vz
    w12 = co(C_W12)
    jx = w12 * (m1x + 3.0 * vx - ux * m0) - big * co(C_G) - co(C_KX) * m1x
    jy = w12 * (m1y + 3.0 * vy - uy * m0) - big * co(C_G + 1)
    jz = w12 * (m1z + 3.0 * vz - uz * m0) - big * co(C_G + 2)
    r = co(C_UU) * m0 - co(C_W8) * uv + co(C_KXU) * m1x - big * co(C_RM)
    omb = co(C_OMB)
    odd = (jx, jy, jz, jx + jy, jx - jy, jx + jz, jx - jz, jy + jz, jy - jz)
    lam = [omb * mu[0] + r]
    for p in range(9):
        even = r + big * co(C_Q + p)
        lam.append(omb * mu[2 * p + 1] + (even + odd[p]))
        lam.append(omb * mu[2 * p + 2] + (even - odd[p]))
    return lam, m1x


def kernel(
    dims,
    thrust_hbm,
    pops_hbm,
    scale_hbm,
    seed_hbm,
    map_hbm,
    out_ref,
    grad_ref,
    pops,
    scale,
    thrust_ref,
    tmap,
    lam,
    halo_y,
    coef,
    gm,
    gmy,
    acc,
    push,
    rows,
    kfield,
    red,
    in_sem,
    send_sem,
    recv_sem,
    gsend_sem,
    grecv_sem,
    rsend_sem,
    rrecv_sem,
    relay_x,
    relay_c,
    prelay_sem,
    frelay_sem,
    ready_sem,
):
    n_gx, n_gy = dims
    gx = lax.axis_index("gx")
    gy = lax.axis_index("gy")
    steps = 3

    right, left = lax.rem(gx + 1, n_gx), lax.rem(gx + n_gx - 1, n_gx)
    up, down = lax.rem(gy + 1, n_gy), lax.rem(gy + n_gy - 1, n_gy)
    around = (
        (left, gy),
        (right, gy),
        (gx, down),
        (gx, up),
        (left, down),
        (right, up),
        (left, up),
        (right, down),
    )
    low_size = CORES * Z_CHIPS
    low = lax.rem(gx, low_size)
    high = gx // low_size
    core = lax.rem(low, CORES)
    z = low // CORES
    yl = lax.rem(gy, Y_LO)
    xc = gy // Y_LO

    def x_peer(j):
        return high * low_size + z * CORES + lax.rem(j, CORES), j // CORES * Y_LO + yl

    def z_peer(j):
        return high * low_size + j * CORES + core, gy

    def y_peer(j):
        return j // Y_LO * low_size + low, xc * Y_LO + lax.rem(j, Y_LO)

    phases = (
        (y_peer, high * Y_LO + yl, n_gx // low_size * Y_LO),
        (x_peer, xc * CORES + core, n_gy // Y_LO * CORES),
        (z_peer, z, Z_CHIPS),
    )

    def far(size):
        return sorted(range(1, size), key=lambda d: abs(d - size // 2))

    is_first, is_relay, is_last = low == 0, low == 1, low == low_size - 1
    relayed = (0, 4, 6)
    relay_from = [(lax.rem(gx + low_size - 1, n_gx), other) for other in (gy, up, down)]
    relay_to = (gx + low_size - 2, gy)

    barrier = pltpu.get_barrier_semaphore()
    far_first = (4, 5, 6, 7, 0, 1, 2, 3)

    def greet(device):
        pl.semaphore_signal(barrier, inc=1, device_id=device, device_id_type=MESH)

    @pl.when(is_relay)
    def _():
        for device in relay_from:
            greet(device)

    @pl.when(is_last)
    def _():
        greet((gx - (low_size - 2), gy))

    @pl.when(jnp.logical_not(is_last))
    def _():
        for i in (5, 7, 1):
            greet(around[i])

    for i in (4, 6, 0, 2, 3):
        greet(around[i])

    loads = [pltpu.make_async_copy(map_hbm, tmap, in_sem.at[0])]
    loads.append(pltpu.make_async_copy(scale_hbm, scale, in_sem.at[1]))
    for t in (2, 1, 0):
        loads.append(pltpu.make_async_copy(pops_hbm.at[t], pops.at[t], in_sem.at[2 + t]))
    for position, member in enumerate(SLOTS):
        loads.append(
            pltpu.make_async_copy(
                seed_hbm.at[member], lam.at[0, position, pl.ds(1, 4)], in_sem.at[5 + position]
            )
        )
    loads.append(pltpu.make_async_copy(thrust_hbm, thrust_ref, in_sem.at[25]))
    for copy in loads:
        copy.start()

    count = 8 + jnp.where(is_relay, 1, 0)
    for peer, mine, size in phases:
        lax.fori_loop(mine + 1, size, lambda j, _, peer=peer: (greet(peer(j)), 0)[1], 0)
        count = count + mine

    shape = (8, 128)
    row = lax.broadcasted_iota(jnp.int32, shape, 0)
    lane = lax.broadcasted_iota(jnp.int32, shape, 1)
    row_one = lax.broadcasted_iota(jnp.int32, (1, 128), 1)

    for copy in loads[5:-1]:
        copy.wait()
    pl.semaphore_wait(barrier, count)

    def halo_copies(e):
        parts = (
            (lam.at[e, 0:5, 1], lam.at[e, 0:5, 5]),
            (lam.at[e, 8:13, 4], lam.at[e, 8:13, 0]),
            (lam.at[e, 4:9, 1:5, 0:1], halo_y.at[e, 0, :, 1:5]),
            (lam.at[e, 12:17, 1:5, 7:8], halo_y.at[e, 1, :, 1:5]),
            (lam.at[e, 4, 1, 0:1], halo_y.at[e, 0, 0, 5]),
            (lam.at[e, 12, 4, 7:8], halo_y.at[e, 1, 0, 0]),
            (lam.at[e, 0, 1, 7:8], halo_y.at[e, 1, 4, 5]),
            (lam.at[e, 8, 4, 0:1], halo_y.at[e, 0, 4, 0]),
        )
        return [
            pltpu.make_async_remote_copy(
                src_ref=src,
                dst_ref=dst,
                send_sem=send_sem.at[e * 8 + i],
                recv_sem=recv_sem.at[e * 8 + i],
                device_id=around[i],
                device_id_type=MESH,
            )
            for i, (src, dst) in enumerate(parts)
        ]

    def field_copies():
        parts = (
            (gm.at[:, 1], gm.at[:, 5]),
            (gm.at[:, 4], gm.at[:, 0]),
            (gm.at[:, 1:5, 0:1], gmy.at[0, :, 1:5]),
            (gm.at[:, 1:5, 7:8], gmy.at[1, :, 1:5]),
            (gm.at[:, 1, 0:1], gmy.at[0, :, 5]),
            (gm.at[:, 4, 7:8], gmy.at[1, :, 0]),
            (gm.at[:, 1, 7:8], gmy.at[1, :, 5]),
            (gm.at[:, 4, 0:1], gmy.at[0, :, 0]),
        )
        return [
            pltpu.make_async_remote_copy(
                src_ref=src,
                dst_ref=dst,
                send_sem=gsend_sem.at[i],
                recv_sem=grecv_sem.at[i],
                device_id=around[i],
                device_id_type=MESH,
            )
            for i, (src, dst) in enumerate(parts)
        ]

    exchanges = [halo_copies(e) for e in range(steps)]
    fields = field_copies()
    parked = (relay_x, relay_c.at[0], relay_c.at[1])

    def relay_copy(k, src, device):
        return pltpu.make_async_remote_copy(
            src_ref=src,
            dst_ref=parked[k],
            send_sem=send_sem.at[relayed[k]],
            recv_sem=prelay_sem.at[k],
            device_id=device,
            device_id_type=MESH,
        )

    sources = (lam.at[0, 0:5, 1], lam.at[0, 4, 1, 0:1], lam.at[0, 0, 1, 7:8])
    landings = (lam.at[0, 0:5, 5], halo_y.at[0, 0, 0, 5], halo_y.at[0, 1, 4, 5])
    inbound = []
    forwards = []
    for k, i in enumerate(relayed):
        device = around[i]
        inbound.append(relay_copy(k, sources[k], (device[0] - (low_size - 2), device[1])))
        forwards.append(
            pltpu.make_async_remote_copy(
                src_ref=parked[k],
                dst_ref=landings[k],
                send_sem=frelay_sem.at[k],
                recv_sem=recv_sem.at[i],
                device_id=relay_to,
                device_id_type=MESH,
            )
        )

    @pl.when(is_first)
    def _():
        for k in (1, 2, 0):
            inbound[k].start()

    @pl.when(jnp.logical_not(is_first))
    def _():
        for i in (4, 6, 0):
            exchanges[0][i].start()

    for i in (5, 7, 1, 2, 3):
        exchanges[0][i].start()
    for phase, (peer, mine, _) in enumerate(phases):

        def answer(j, _, phase=phase, peer=peer):
            pl.semaphore_signal(
                ready_sem.at[phase], inc=1, device_id=peer(j), device_id_type=MESH
            )
            return 0

        lax.fori_loop(0, mine, answer, 0)

    @pl.when(is_relay)
    def _():
        for k in (1, 2, 0):
            inbound[k].wait_recv()
        for k in (1, 2, 0):
            forwards[k].start()

    loads[0].wait()
    loads[-1].wait()

    turbines = thrust_ref.shape[0]

    def fill(x, _):
        ids = tmap[x]
        value = jnp.zeros(shape, F32)
        for m in range(turbines):
            value = jnp.where(ids == m, thrust_ref[m], value)
        side = 1.0 + jnp.sqrt(1.0 - value)
        kfield[x] = 4.0 * value / (side * side)
        gm[1, x + 1] = ids.astype(F32)
        acc[x] = jnp.zeros(shape, F32)
        return 0

    lax.fori_loop(0, 4, fill, 0)
    loads[1].wait()
    for t in (2, 1, 0):
        loads[2 + (2 - t)].wait()

    def prepare(i, _):
        t = i // 4
        x = lax.rem(i, 4)
        values = coefficients(
            [pops[t, member, x].astype(F32) for member in range(19)], scale[t, x], kfield[x]
        )
        for j, value in enumerate(values):
            coef[t, x, j] = value
        return 0

    lax.fori_loop(0, 12, prepare, 0)
    for x in range(4):
        gm[0, x + 1] = coef[0, x, C_GK]

    def streamed(e, x):
        mu = []
        for member in range(19):
            cx, cy, cz = VELOCITIES[member]
            value = lam[e, SLOT[member], x + cx]
            if cy != 0:
                value = pltpu.roll(value, 7 if cy == 1 else 1, 0)
                side, group = (0, YP) if cy == 1 else (1, YM)
                edge = halo_y[e, side, group.index(member), x + cx]
                value = jnp.where(row == (7 if cy == 1 else 0), jnp.broadcast_to(edge, shape), value)
            if cz != 0:
                value = pltpu.roll(value, 127 if cz == 1 else 1, 1)
                value = jnp.where(
                    lane == (127 if cz == 1 else 0), lam[e, SLOT[OPPOSITE[member]], x], value
                )
            mu.append(value)
        return mu

    def plane(e, x):
        t = 2 - e
        result, m1x = transposed(streamed(e, x), lambda j: coef[t, x - 1, j])
        if e < 2:
            for position, member in enumerate(SLOTS):
                lam[e + 1, position, x] = result[member]
            acc[x - 1] += m1x * coef[t, x - 1, C_GK]
        else:
            for member in range(19):
                out_ref[member, x - 1] = result[member]
        return result

    def push_plane(x, value):
        zero = jnp.zeros(shape, F32)
        top, bottom = lane == 127, lane == 0
        first, last = row == 0, row == 7

        def lower(v):
            return jnp.where(top, zero, pltpu.roll(v, 127, 1))

        def raise_(v):
            return jnp.where(bottom, zero, pltpu.roll(v, 1, 1))

        push[0, x] = (
            (value[1] + value[1])
            + lower(value[11])
            + raise_(value[13])
            + jnp.where(last, zero, pltpu.roll(value[7], 7, 0))
            + jnp.where(first, zero, pltpu.roll(value[9], 1, 0))
        )
        push[1, x] = -(
            (value[2] + value[2])
            + raise_(value[12])
            + lower(value[14])
            + jnp.where(first, zero, pltpu.roll(value[8], 1, 0))
            + jnp.where(last, zero, pltpu.roll(value[10], 7, 0))
        )
        push[2, x] = jnp.where(top, value[12] - value[13], zero) + jnp.where(
            bottom, value[14] - value[11], zero
        )
        rows[0, 0, pl.ds(x - 1, 1), :] = value[7][0:1]
        rows[0, 1, pl.ds(x + 1, 1), :] = value[10][0:1]
        rows[1, 0, pl.ds(x - 1, 1), :] = value[9][7:8]
        rows[1, 1, pl.ds(x + 1, 1), :] = value[8][7:8]

    rows[...] = jnp.zeros((2, 2, 8, 128), F32)

    def step(e):
        for i in (2, 3):
            exchanges[e][i].wait_recv()

        def inner(i, _):
            result = plane(e, 2 + i)
            if e == 1:
                push_plane(2 + i, result)
            return 0

        lax.fori_loop(0, 2, inner, 0)
        for i in (0, 1, 4, 5, 6, 7):
            exchanges[e][i].wait_recv()

        def outer(i, _):
            result = plane(e, 1 + 3 * i)
            if e == 1:
                push_plane(1 + 3 * i, result)
            return 0

        lax.fori_loop(0, 2, outer, 0)
        if e < 2:
            for i in far_first:
                exchanges[e + 1][i].start()

    step(0)
    for i in far_first:
        fields[i].start()
    step(1)

    for copy in fields:
        copy.wait_recv()
    zero = jnp.zeros(shape, F32)
    weights, ids = [], []
    for x in range(6):
        value = zero
        if x + 1 <= 4:
            value = value + push[0, x + 1]
        if x - 1 >= 1:
            value = value + push[1, x - 1]
        if 1 <= x <= 4:
            value = (value + push[2, x]) * gm[0, x] + acc[x - 1]
        else:
            value = value * gm[0, x]
        weights.append(value)
        ids.append(gm[1, x])
    for side in range(2):
        value = rows[side, 0] - rows[side, 1]
        g = jnp.concatenate([gmy[1 - side, 0, x] for x in range(6)] + [jnp.zeros((2, 128), F32)], 0)
        m = jnp.concatenate([gmy[1 - side, 1, x] for x in range(6)] + [jnp.full((2, 128), -1.0, F32)], 0)
        weights.append(value * g)
        ids.append(m)
    collected = zero
    for m in range(turbines):
        part = total(jnp.where(ids[i] == float(m), weights[i], zero) for i in range(8))
        collected = jnp.where(lane == m, jnp.sum(part, axis=1, keepdims=True), collected)
    partial = jnp.sum(collected, axis=0, keepdims=True)

    reduced = []
    copies = []
    for phase, (peer, mine, size) in enumerate(phases):
        red[phase, mine] = partial
        started = []
        @pl.when(mine < size - 1)
        def _():
            pl.semaphore_wait(ready_sem.at[phase], size - 1 - mine)

        for d in far(size):
            device = peer(lax.rem(mine + d, size))
            started.append(
                pltpu.make_async_remote_copy(
                    src_ref=red.at[phase, mine],
                    dst_ref=red.at[phase, mine],
                    send_sem=rsend_sem.at[phase, d],
                    recv_sem=rrecv_sem.at[phase, d],
                    device_id=device,
                    device_id_type=MESH,
                )
            )
        for copy in started:
            copy.start()
        copies += started
        if phase == len(phases) - 1:
            step(2)
        for copy in started:
            copy.wait_recv()
        partial = total(red[phase, j] for j in range(size))

    thrust = jnp.zeros((1, 128), F32)
    for m in range(turbines):
        thrust = jnp.where(row_one == m, thrust_ref[m], thrust)
    side = jnp.sqrt(1.0 - thrust)
    slope = 4.0 / (side * ((1.0 + side) * (1.0 + side)))
    grad_ref[...] = (partial * slope)[0, 0:turbines]

    for group in exchanges + [fields, copies]:
        for copy in group:
            copy.wait_send()

    @pl.when(is_relay)
    def _():
        for copy in forwards:
            copy.wait_send()


def write_kernel(adjoint_vmem, grad_vmem, adjoint_out, grad_out, sem):
    copies = (
        pltpu.make_async_copy(adjoint_vmem, adjoint_out, sem.at[0]),
        pltpu.make_async_copy(grad_vmem, grad_out, sem.at[1]),
    )
    for copy in copies:
        copy.start()
    for copy in copies:
        copy.wait()


def shards(n_gx, n_gy, fwd_pops, fwd_scale, seed_adjoint, turbine_map, thrust):
    phase_max = max(Z_CHIPS, n_gx // (Z_CHIPS * CORES) * Y_LO, n_gy // Y_LO * CORES)
    hbm = pl.BlockSpec(memory_space=pl.ANY)
    vmem = pl.BlockSpec(memory_space=pltpu.VMEM)
    results = pl.pallas_call(
        functools.partial(kernel, (n_gx, n_gy)),
        out_shape=(pltpu.VMEM(seed_adjoint.shape, F32), pltpu.VMEM(thrust.shape, F32)),
        in_specs=[hbm, hbm, hbm, hbm, hbm],
        out_specs=(vmem, vmem),
        scratch_shapes=[
            pltpu.VMEM(fwd_pops.shape, fwd_pops.dtype),
            pltpu.VMEM(fwd_scale.shape, F32),
            pltpu.SMEM(thrust.shape, F32),
            pltpu.VMEM(turbine_map.shape, jnp.int32),
            pltpu.VMEM((3, 20, 6, 8, 128), F32),
            pltpu.VMEM((3, 2, 5, 6, 1, 128), F32),
            pltpu.VMEM((3, 4, N_COEF, 8, 128), F32),
            pltpu.VMEM((2, 6, 8, 128), F32),
            pltpu.VMEM((2, 2, 6, 1, 128), F32),
            pltpu.VMEM((4, 8, 128), F32),
            pltpu.VMEM((3, 5, 8, 128), F32),
            pltpu.VMEM((2, 2, 8, 128), F32),
            pltpu.VMEM((4, 8, 128), F32),
            pltpu.VMEM((3, phase_max, 1, 128), F32),
            pltpu.SemaphoreType.DMA((26,)),
            pltpu.SemaphoreType.DMA((24,)),
            pltpu.SemaphoreType.DMA((24,)),
            pltpu.SemaphoreType.DMA((8,)),
            pltpu.SemaphoreType.DMA((8,)),
            pltpu.SemaphoreType.DMA((3, phase_max)),
            pltpu.SemaphoreType.DMA((3, phase_max)),
            pltpu.VMEM((5, 8, 128), F32),
            pltpu.VMEM((2, 1, 128), F32),
            pltpu.SemaphoreType.DMA((3,)),
            pltpu.SemaphoreType.DMA((3,)),
            pltpu.SemaphoreType.REGULAR((3,)),
        ],
        compiler_params=pltpu.CompilerParams(collective_id=0, has_side_effects=True),
        name="adjoint",
    )(thrust, fwd_pops, fwd_scale, seed_adjoint, turbine_map)
    return pl.pallas_call(
        write_kernel,
        out_shape=(
            jax.ShapeDtypeStruct(seed_adjoint.shape, F32),
            jax.ShapeDtypeStruct(thrust.shape, F32),
        ),
        in_specs=[vmem, vmem],
        out_specs=(hbm, hbm),
        scratch_shapes=[pltpu.SemaphoreType.DMA((2,))],
        name="write",
    )(*[pltpu.with_memory_space_constraint(r, pltpu.VMEM) for r in results])


def solution(mesh):
    placed = (
        P(None, None, "gx", "gy", None),
        P(None, "gx", "gy", None),
        P(None, "gx", "gy", None),
        P("gx", "gy", None),
        P(),
    )
    return jax.shard_map(
        functools.partial(shards, mesh.shape["gx"], mesh.shape["gy"]),
        mesh=mesh,
        in_specs=placed,
        out_specs=(P(None, "gx", "gy", None), P()),
        check_vma=False,
    )
```

```python
import functools

import jax
import jax.numpy as jnp
from jax import lax
from jax.experimental import pallas as pl
from jax.experimental.pallas import tpu as pltpu
from jax.sharding import PartitionSpec as P

MESH = pl.DeviceIdType.MESH
F32 = jnp.float32

VELOCITIES = (
    (0, 0, 0),
    (1, 0, 0),
    (-1, 0, 0),
    (0, 1, 0),
    (0, -1, 0),
    (0, 0, 1),
    (0, 0, -1),
    (1, 1, 0),
    (-1, -1, 0),
    (1, -1, 0),
    (-1, 1, 0),
    (1, 0, 1),
    (-1, 0, -1),
    (1, 0, -1),
    (-1, 0, 1),
    (0, 1, 1),
    (0, -1, -1),
    (0, 1, -1),
    (0, -1, 1),
)
OPPOSITE = (0, 2, 1, 4, 3, 6, 5, 8, 7, 10, 9, 12, 11, 14, 13, 16, 15, 18, 17)
WEIGHTS = tuple([1.0 / 3.0] + [1.0 / 18.0] * 6 + [1.0 / 36.0] * 12)
MEAN_FLOW = 0.1
TAU_BASE = 0.51
SMAG_COEF = 18.0 * 1.4142135623730951 * 0.17 * 0.17
QUAD_FLOOR = 0.0001

SLOTS = (9, 1, 11, 13, 7, 3, 15, 17, 10, 2, 12, 14, 8, 4, 16, 18, 9, 0, 5, 6)
SLOT = {member: SLOTS.index(member) for member in range(19)}
YP = SLOTS[4:9]
YM = SLOTS[12:17]
CORES = 2
Z_CHIPS = 8
Y_LO = 2

C_N = 0
C_Q = 19
C_G = 28
C_U = 31
C_RM, C_OMB, C_W12, C_UU, C_W8, C_KX, C_KXU, C_GK = range(34, 42)
N_COEF = 42


def base_values():
    values = []
    for member in range(19):
        along = float(VELOCITIES[member][0])
        values.append(
            WEIGHTS[member]
            * (
                1.0
                + 3.0 * MEAN_FLOW * along
                + 4.5 * MEAN_FLOW * MEAN_FLOW * along * along
                - 1.5 * MEAN_FLOW * MEAN_FLOW
            )
        )
    return values


def total(terms):
    terms = list(terms)
    while len(terms) > 1:
        terms = [
            terms[i] + terms[i + 1] if i + 1 < len(terms) else terms[i]
            for i in range(0, len(terms), 2)
        ]
    return terms[0]


def second_moments(pair):
    sx, sy, sz, a, b, c, d, e, f = pair
    txy, txz, tyz = a + b, c + d, e + f
    return sx, sy, sz, txy, txz, tyz, a - b, c - d, e - f


def coefficients(pops, scale, k):
    base = base_values()
    f = [base[i] + (base[i] * scale) * pops[i] for i in range(19)]
    rho = total(f)
    sums = [f[2 * p + 1] + f[2 * p + 2] for p in range(9)]
    difs = [f[2 * p + 1] - f[2 * p + 2] for p in range(9)]
    jx = (difs[0] + difs[3] + difs[4]) + (difs[5] + difs[6])
    jy = (difs[1] + difs[3] - difs[4]) + (difs[7] + difs[8])
    jz = (difs[2] + difs[5] - difs[6]) + (difs[7] - difs[8])
    inv = 1.0 / rho
    u = (jx * inv, jy * inv, jz * inv)
    u2 = u[0] * u[0] + u[1] * u[1] + u[2] * u[2]
    rest = 1.0 - 1.5 * u2
    n = [None] * 19
    third = rho * (1.0 / 3.0)
    n[0] = f[0] - third * rest
    r18 = rho * (1.0 / 18.0)
    r36 = rho * (1.0 / 36.0)
    proj = (
        u[0],
        u[1],
        u[2],
        u[0] + u[1],
        u[0] - u[1],
        u[0] + u[2],
        u[0] - u[2],
        u[1] + u[2],
        u[1] - u[2],
    )
    for p in range(9):
        even = rest + 4.5 * (proj[p] * proj[p])
        odd = 3.0 * proj[p]
        weight = r18 if p < 3 else r36
        n[2 * p + 1] = f[2 * p + 1] - weight * (even + odd)
        n[2 * p + 2] = f[2 * p + 2] - weight * (even - odd)
    pair = [n[2 * p + 1] + n[2 * p + 2] for p in range(9)]
    sx, sy, sz, txy, txz, tyz, pxy, pxz, pyz = second_moments(pair)
    pxx = sx + txy + txz
    pyy = sy + txy + tyz
    pzz = sz + txz + tyz
    square = (pxx * pxx + pyy * pyy + pzz * pzz) + 2.0 * (
        pxy * pxy + pxz * pxz + pyz * pyz
    )
    q = jnp.sqrt(square + QUAD_FLOOR)
    s = jnp.sqrt(TAU_BASE * TAU_BASE + SMAG_COEF * (q * inv))
    om = 2.0 / (TAU_BASE + s)
    a1 = (om * om) * (0.25 * SMAG_COEF) * inv / (s * q)
    a2 = a1 * (q * q) * inv
    pu = (
        pxx * u[0] + pxy * u[1] + pxz * u[2],
        pxy * u[0] + pyy * u[1] + pyz * u[2],
        pxz * u[0] + pyz * u[1] + pzz * u[2],
    )
    upu = u[0] * pu[0] + u[1] * pu[1] + u[2] * pu[2]
    trace = pxx + pyy + pzz
    quads = (
        pxx,
        pyy,
        pzz,
        pxx + pyy + 2.0 * pxy,
        pxx + pyy - 2.0 * pxy,
        pxx + pzz + 2.0 * pxz,
        pxx + pzz - 2.0 * pxz,
        pyy + pzz + 2.0 * pyz,
        pyy + pzz - 2.0 * pyz,
    )
    absu = jnp.abs(u[0])
    kx = k * absu * inv * (1.0 / 12.0)
    out = list(n)
    out += [a1 * value for value in quads]
    out += [(2.0 * a1) * value for value in pu]
    out += list(u)
    out += [
        a2 + a1 * (trace * (1.0 / 3.0) - upu),
        1.0 - om,
        om * (1.0 / 12.0),
        om * (1.0 / 36.0) * (1.0 + 1.5 * u2),
        om * 0.125,
        kx,
        kx * u[0],
        (-1.5 / 36.0) * (u[0] * absu),
    ]
    return out


def transposed(mu, co):
    sums = [mu[2 * p + 1] + mu[2 * p + 2] for p in range(9)]
    difs = [mu[2 * p + 1] - mu[2 * p + 2] for p in range(9)]
    sx, sy, sz, txy, txz, tyz, mxy, mxz, myz = second_moments(sums)
    sx, sy, sz = sx + sx, sy + sy, sz + sz
    mxx = sx + txy + txz
    myy = sy + txy + tyz
    mzz = sz + txz + tyz
    m0 = 12.0 * mu[0] + ((sx + sy + sz) + (txy + txz + tyz))
    m1x = (difs[0] + difs[0]) + (difs[3] + difs[4]) + (difs[5] + difs[6])
    m1y = (difs[1] + difs[1]) + (difs[3] - difs[4]) + (difs[7] + difs[8])
    m1z = (difs[2] + difs[2]) + (difs[5] - difs[6]) + (difs[7] - difs[8])
    big = total(mu[i] * co(C_N + i) for i in range(19))
    ux, uy, uz = co(C_U), co(C_U + 1), co(C_U + 2)
    vx = mxx * ux + mxy * uy + mxz * uz
    vy = mxy * ux + myy * uy + myz * uz
    vz = mxz * ux + myz * uy + mzz * uz
    uv = ux * vx + uy * vy + uz * vz
    w12 = co(C_W12)
    jx = w12 * (m1x + 3.0 * vx - ux * m0) - big * co(C_G) - co(C_KX) * m1x
    jy = w12 * (m1y + 3.0 * vy - uy * m0) - big * co(C_G + 1)
    jz = w12 * (m1z + 3.0 * vz - uz * m0) - big * co(C_G + 2)
    r = co(C_UU) * m0 - co(C_W8) * uv + co(C_KXU) * m1x - big * co(C_RM)
    omb = co(C_OMB)
    odd = (jx, jy, jz, jx + jy, jx - jy, jx + jz, jx - jz, jy + jz, jy - jz)
    lam = [omb * mu[0] + r]
    for p in range(9):
        even = r + big * co(C_Q + p)
        lam.append(omb * mu[2 * p + 1] + (even + odd[p]))
        lam.append(omb * mu[2 * p + 2] + (even - odd[p]))
    return lam, m1x


def kernel(
    dims,
    thrust_hbm,
    pops_hbm,
    scale_hbm,
    seed_hbm,
    map_hbm,
    out_ref,
    grad_ref,
    pops,
    scale,
    thrust_ref,
    tmap,
    lam,
    halo_y,
    coef,
    gm,
    gmy,
    acc,
    push,
    rows,
    kfield,
    red,
    in_sem,
    send_sem,
    recv_sem,
    gsend_sem,
    grecv_sem,
    rsend_sem,
    rrecv_sem,
    relay_x,
    relay_c,
    prelay_sem,
    frelay_sem,
    ready_sem,
):
    n_gx, n_gy = dims
    gx = lax.axis_index("gx")
    gy = lax.axis_index("gy")
    steps = 3

    right, left = lax.rem(gx + 1, n_gx), lax.rem(gx + n_gx - 1, n_gx)
    up, down = lax.rem(gy + 1, n_gy), lax.rem(gy + n_gy - 1, n_gy)
    around = (
        (left, gy),
        (right, gy),
        (gx, down),
        (gx, up),
        (left, down),
        (right, up),
        (left, up),
        (right, down),
    )
    low_size = CORES * Z_CHIPS
    low = lax.rem(gx, low_size)
    high = gx // low_size
    core = lax.rem(low, CORES)
    z = low // CORES
    yl = lax.rem(gy, Y_LO)
    xc = gy // Y_LO

    def x_peer(j):
        return high * low_size + z * CORES + lax.rem(j, CORES), j // CORES * Y_LO + yl

    def z_peer(j):
        return high * low_size + j * CORES + core, gy

    def y_peer(j):
        return j // Y_LO * low_size + low, xc * Y_LO + lax.rem(j, Y_LO)

    phases = (
        (y_peer, high * Y_LO + yl, n_gx // low_size * Y_LO),
        (x_peer, xc * CORES + core, n_gy // Y_LO * CORES),
        (z_peer, z, Z_CHIPS),
    )

    def far(size):
        return sorted(range(1, size), key=lambda d: abs(d - size // 2))

    is_first, is_relay, is_last = low == 0, low == 1, low == low_size - 1
    relayed = (0, 4, 6)
    relay_from = [(lax.rem(gx + low_size - 1, n_gx), other) for other in (gy, up, down)]
    relay_to = (gx + low_size - 2, gy)

    barrier = pltpu.get_barrier_semaphore()
    far_first = (4, 5, 6, 7, 0, 1, 2, 3)

    def greet(device):
        pl.semaphore_signal(barrier, inc=1, device_id=device, device_id_type=MESH)

    @pl.when(is_relay)
    def _():
        for device in relay_from:
            greet(device)

    @pl.when(is_last)
    def _():
        greet((gx - (low_size - 2), gy))

    @pl.when(jnp.logical_not(is_last))
    def _():
        for i in (5, 7, 1):
            greet(around[i])

    for i in (4, 6, 0, 2, 3):
        greet(around[i])

    loads = [pltpu.make_async_copy(map_hbm, tmap, in_sem.at[0])]
    loads.append(pltpu.make_async_copy(scale_hbm, scale, in_sem.at[1]))
    for t in (2, 1, 0):
        loads.append(pltpu.make_async_copy(pops_hbm.at[t], pops.at[t], in_sem.at[2 + t]))
    for position, member in enumerate(SLOTS):
        loads.append(
            pltpu.make_async_copy(
                seed_hbm.at[member], lam.at[0, position, pl.ds(1, 4)], in_sem.at[5 + position]
            )
        )
    loads.append(pltpu.make_async_copy(thrust_hbm, thrust_ref, in_sem.at[25]))
    for copy in loads:
        copy.start()

    count = 8 + jnp.where(is_relay, 1, 0)
    for peer, mine, size in phases:
        lax.fori_loop(mine + 1, size, lambda j, _, peer=peer: (greet(peer(j)), 0)[1], 0)
        count = count + mine

    shape = (8, 128)
    row = lax.broadcasted_iota(jnp.int32, shape, 0)
    lane = lax.broadcasted_iota(jnp.int32, shape, 1)
    row_one = lax.broadcasted_iota(jnp.int32, (1, 128), 1)

    for copy in loads[5:-1]:
        copy.wait()
    pl.semaphore_wait(barrier, count)

    def halo_copies(e):
        parts = (
            (lam.at[e, 0:5, 1], lam.at[e, 0:5, 5]),
            (lam.at[e, 8:13, 4], lam.at[e, 8:13, 0]),
            (lam.at[e, 4:9, 1:5, 0:1], halo_y.at[e, 0, :, 1:5]),
            (lam.at[e, 12:17, 1:5, 7:8], halo_y.at[e, 1, :, 1:5]),
            (lam.at[e, 4, 1, 0:1], halo_y.at[e, 0, 0, 5]),
            (lam.at[e, 12, 4, 7:8], halo_y.at[e, 1, 0, 0]),
            (lam.at[e, 0, 1, 7:8], halo_y.at[e, 1, 4, 5]),
            (lam.at[e, 8, 4, 0:1], halo_y.at[e, 0, 4, 0]),
        )
        return [
            pltpu.make_async_remote_copy(
                src_ref=src,
                dst_ref=dst,
                send_sem=send_sem.at[e * 8 + i],
                recv_sem=recv_sem.at[e * 8 + i],
                device_id=around[i],
                device_id_type=MESH,
            )
            for i, (src, dst) in enumerate(parts)
        ]

    def field_copies():
        parts = (
            (gm.at[:, 1], gm.at[:, 5]),
            (gm.at[:, 4], gm.at[:, 0]),
            (gm.at[:, 1:5, 0:1], gmy.at[0, :, 1:5]),
            (gm.at[:, 1:5, 7:8], gmy.at[1, :, 1:5]),
            (gm.at[:, 1, 0:1], gmy.at[0, :, 5]),
            (gm.at[:, 4, 7:8], gmy.at[1, :, 0]),
            (gm.at[:, 1, 7:8], gmy.at[1, :, 5]),
            (gm.at[:, 4, 0:1], gmy.at[0, :, 0]),
        )
        return [
            pltpu.make_async_remote_copy(
                src_ref=src,
                dst_ref=dst,
                send_sem=gsend_sem.at[i],
                recv_sem=grecv_sem.at[i],
                device_id=around[i],
                device_id_type=MESH,
            )
            for i, (src, dst) in enumerate(parts)
        ]

    exchanges = [halo_copies(e) for e in range(steps)]
    fields = field_copies()
    parked = (relay_x, relay_c.at[0], relay_c.at[1])

    def relay_copy(k, src, device):
        return pltpu.make_async_remote_copy(
            src_ref=src,
            dst_ref=parked[k],
            send_sem=send_sem.at[relayed[k]],
            recv_sem=prelay_sem.at[k],
            device_id=device,
            device_id_type=MESH,
        )

    sources = (lam.at[0, 0:5, 1], lam.at[0, 4, 1, 0:1], lam.at[0, 0, 1, 7:8])
    landings = (lam.at[0, 0:5, 5], halo_y.at[0, 0, 0, 5], halo_y.at[0, 1, 4, 5])
    inbound = []
    forwards = []
    for k, i in enumerate(relayed):
        device = around[i]
        inbound.append(relay_copy(k, sources[k], (device[0] - (low_size - 2), device[1])))
        forwards.append(
            pltpu.make_async_remote_copy(
                src_ref=parked[k],
                dst_ref=landings[k],
                send_sem=frelay_sem.at[k],
                recv_sem=recv_sem.at[i],
                device_id=relay_to,
                device_id_type=MESH,
            )
        )

    @pl.when(is_first)
    def _():
        for k in (1, 2, 0):
            inbound[k].start()

    @pl.when(jnp.logical_not(is_first))
    def _():
        for i in (4, 6, 0):
            exchanges[0][i].start()

    for i in (5, 7, 1, 2, 3):
        exchanges[0][i].start()
    for phase, (peer, mine, _) in enumerate(phases):

        def answer(j, _, phase=phase, peer=peer):
            pl.semaphore_signal(
                ready_sem.at[phase], inc=1, device_id=peer(j), device_id_type=MESH
            )
            return 0

        lax.fori_loop(0, mine, answer, 0)

    @pl.when(is_relay)
    def _():
        for k in (1, 2, 0):
            inbound[k].wait_recv()
        for k in (1, 2, 0):
            forwards[k].start()

    loads[0].wait()
    loads[-1].wait()

    turbines = thrust_ref.shape[0]

    def fill(x, _):
        ids = tmap[x]
        value = jnp.zeros(shape, F32)
        for m in range(turbines):
            value = jnp.where(ids == m, thrust_ref[m], value)
        side = 1.0 + jnp.sqrt(1.0 - value)
        kfield[x] = 4.0 * value / (side * side)
        gm[1, x + 1] = ids.astype(F32)
        acc[x] = jnp.zeros(shape, F32)
        return 0

    lax.fori_loop(0, 4, fill, 0)
    loads[1].wait()
    for t in (2, 1, 0):
        loads[2 + (2 - t)].wait()

    def prepare(i, _):
        t = i // 4
        x = lax.rem(i, 4)
        values = coefficients(
            [pops[t, member, x].astype(F32) for member in range(19)], scale[t, x], kfield[x]
        )
        for j, value in enumerate(values):
            coef[t, x, j] = value
        return 0

    lax.fori_loop(0, 12, prepare, 0)
    for x in range(4):
        gm[0, x + 1] = coef[0, x, C_GK]

    def streamed(e, x):
        mu = []
        for member in range(19):
            cx, cy, cz = VELOCITIES[member]
            value = lam[e, SLOT[member], x + cx]
            if cy != 0:
                value = pltpu.roll(value, 7 if cy == 1 else 1, 0)
                side, group = (0, YP) if cy == 1 else (1, YM)
                edge = halo_y[e, side, group.index(member), x + cx]
                value = jnp.where(row == (7 if cy == 1 else 0), jnp.broadcast_to(edge, shape), value)
            if cz != 0:
                value = pltpu.roll(value, 127 if cz == 1 else 1, 1)
                value = jnp.where(
                    lane == (127 if cz == 1 else 0), lam[e, SLOT[OPPOSITE[member]], x], value
                )
            mu.append(value)
        return mu

    def plane(e, x):
        t = 2 - e
        result, m1x = transposed(streamed(e, x), lambda j: coef[t, x - 1, j])
        if e < 2:
            for position, member in enumerate(SLOTS):
                lam[e + 1, position, x] = result[member]
            acc[x - 1] += m1x * coef[t, x - 1, C_GK]
        else:
            for member in range(19):
                out_ref[member, x - 1] = result[member]
        return result

    def push_plane(x, value):
        zero = jnp.zeros(shape, F32)
        top, bottom = lane == 127, lane == 0
        first, last = row == 0, row == 7

        def lower(v):
            return jnp.where(top, zero, pltpu.roll(v, 127, 1))

        def raise_(v):
            return jnp.where(bottom, zero, pltpu.roll(v, 1, 1))

        push[0, x] = (
            (value[1] + value[1])
            + lower(value[11])
            + raise_(value[13])
            + jnp.where(last, zero, pltpu.roll(value[7], 7, 0))
            + jnp.where(first, zero, pltpu.roll(value[9], 1, 0))
        )
        push[1, x] = -(
            (value[2] + value[2])
            + raise_(value[12])
            + lower(value[14])
            + jnp.where(first, zero, pltpu.roll(value[8], 1, 0))
            + jnp.where(last, zero, pltpu.roll(value[10], 7, 0))
        )
        push[2, x] = jnp.where(top, value[12] - value[13], zero) + jnp.where(
            bottom, value[14] - value[11], zero
        )
        rows[0, 0, pl.ds(x - 1, 1), :] = value[7][0:1]
        rows[0, 1, pl.ds(x + 1, 1), :] = value[10][0:1]
        rows[1, 0, pl.ds(x - 1, 1), :] = value[9][7:8]
        rows[1, 1, pl.ds(x + 1, 1), :] = value[8][7:8]

    thrust = jnp.zeros((1, 128), F32)
    for m in range(turbines):
        thrust = jnp.where(row_one == m, thrust_ref[m], thrust)
    side = jnp.sqrt(1.0 - thrust)
    slope = 4.0 / (side * ((1.0 + side) * (1.0 + side)))

    rows[...] = jnp.zeros((2, 2, 8, 128), F32)

    def step(e):
        for i in (2, 3):
            exchanges[e][i].wait_recv()

        def inner(i, _):
            result = plane(e, 2 + i)
            if e == 1:
                push_plane(2 + i, result)
            return 0

        lax.fori_loop(0, 2, inner, 0)
        for i in (0, 1, 4, 5, 6, 7):
            exchanges[e][i].wait_recv()

        def outer(i, _):
            result = plane(e, 1 + 3 * i)
            if e == 1:
                push_plane(1 + 3 * i, result)
            return 0

        lax.fori_loop(0, 2, outer, 0)
        if e < 2:
            for i in far_first:
                exchanges[e + 1][i].start()

    step(0)
    for i in far_first:
        fields[i].start()
    step(1)

    for copy in fields:
        copy.wait_recv()
    zero = jnp.zeros(shape, F32)
    weights, ids = [], []
    for x in range(6):
        value = zero
        if x + 1 <= 4:
            value = value + push[0, x + 1]
        if x - 1 >= 1:
            value = value + push[1, x - 1]
        if 1 <= x <= 4:
            value = (value + push[2, x]) * gm[0, x] + acc[x - 1]
        else:
            value = value * gm[0, x]
        weights.append(value)
        ids.append(gm[1, x])
    for side in range(2):
        value = rows[side, 0] - rows[side, 1]
        g = jnp.concatenate([gmy[1 - side, 0, x] for x in range(6)] + [jnp.zeros((2, 128), F32)], 0)
        m = jnp.concatenate([gmy[1 - side, 1, x] for x in range(6)] + [jnp.full((2, 128), -1.0, F32)], 0)
        weights.append(value * g)
        ids.append(m)
    collected = zero
    for m in range(turbines):
        part = total(jnp.where(ids[i] == float(m), weights[i], zero) for i in range(8))
        collected = jnp.where(lane == m, jnp.sum(part, axis=1, keepdims=True), collected)
    partial = jnp.sum(collected, axis=0, keepdims=True)

    reduced = []
    copies = []
    for phase, (peer, mine, size) in enumerate(phases):
        red[phase, mine] = partial
        started = []
        @pl.when(mine < size - 1)
        def _():
            pl.semaphore_wait(ready_sem.at[phase], size - 1 - mine)

        for d in far(size):
            device = peer(lax.rem(mine + d, size))
            started.append(
                pltpu.make_async_remote_copy(
                    src_ref=red.at[phase, mine],
                    dst_ref=red.at[phase, mine],
                    send_sem=rsend_sem.at[phase, d],
                    recv_sem=rrecv_sem.at[phase, d],
                    device_id=device,
                    device_id_type=MESH,
                )
            )
        for copy in started:
            copy.start()
        copies += started
        if phase == len(phases) - 1:
            step(2)
            for group in exchanges + [fields, copies]:
                for copy in group:
                    copy.wait_send()
        for copy in started:
            copy.wait_recv()
        partial = total(red[phase, j] for j in range(size))

    grad_ref[...] = (partial * slope)[0, 0:turbines]

    @pl.when(is_relay)
    def _():
        for copy in forwards:
            copy.wait_send()


def write_kernel(adjoint_vmem, grad_vmem, adjoint_out, grad_out, sem):
    copies = (
        pltpu.make_async_copy(adjoint_vmem, adjoint_out, sem.at[0]),
        pltpu.make_async_copy(grad_vmem, grad_out, sem.at[1]),
    )
    for copy in copies:
        copy.start()
    for copy in copies:
        copy.wait()


def shards(n_gx, n_gy, fwd_pops, fwd_scale, seed_adjoint, turbine_map, thrust):
    phase_max = max(Z_CHIPS, n_gx // (Z_CHIPS * CORES) * Y_LO, n_gy // Y_LO * CORES)
    hbm = pl.BlockSpec(memory_space=pl.ANY)
    vmem = pl.BlockSpec(memory_space=pltpu.VMEM)
    results = pl.pallas_call(
        functools.partial(kernel, (n_gx, n_gy)),
        out_shape=(pltpu.VMEM(seed_adjoint.shape, F32), pltpu.VMEM(thrust.shape, F32)),
        in_specs=[hbm, hbm, hbm, hbm, hbm],
        out_specs=(vmem, vmem),
        scratch_shapes=[
            pltpu.VMEM(fwd_pops.shape, fwd_pops.dtype),
            pltpu.VMEM(fwd_scale.shape, F32),
            pltpu.SMEM(thrust.shape, F32),
            pltpu.VMEM(turbine_map.shape, jnp.int32),
            pltpu.VMEM((3, 20, 6, 8, 128), F32),
            pltpu.VMEM((3, 2, 5, 6, 1, 128), F32),
            pltpu.VMEM((3, 4, N_COEF, 8, 128), F32),
            pltpu.VMEM((2, 6, 8, 128), F32),
            pltpu.VMEM((2, 2, 6, 1, 128), F32),
            pltpu.VMEM((4, 8, 128), F32),
            pltpu.VMEM((3, 5, 8, 128), F32),
            pltpu.VMEM((2, 2, 8, 128), F32),
            pltpu.VMEM((4, 8, 128), F32),
            pltpu.VMEM((3, phase_max, 1, 128), F32),
            pltpu.SemaphoreType.DMA((26,)),
            pltpu.SemaphoreType.DMA((24,)),
            pltpu.SemaphoreType.DMA((24,)),
            pltpu.SemaphoreType.DMA((8,)),
            pltpu.SemaphoreType.DMA((8,)),
            pltpu.SemaphoreType.DMA((3, phase_max)),
            pltpu.SemaphoreType.DMA((3, phase_max)),
            pltpu.VMEM((5, 8, 128), F32),
            pltpu.VMEM((2, 1, 128), F32),
            pltpu.SemaphoreType.DMA((3,)),
            pltpu.SemaphoreType.DMA((3,)),
            pltpu.SemaphoreType.REGULAR((3,)),
        ],
        compiler_params=pltpu.CompilerParams(collective_id=0, has_side_effects=True),
        name="adjoint",
    )(thrust, fwd_pops, fwd_scale, seed_adjoint, turbine_map)
    return pl.pallas_call(
        write_kernel,
        out_shape=(
            jax.ShapeDtypeStruct(seed_adjoint.shape, F32),
            jax.ShapeDtypeStruct(thrust.shape, F32),
        ),
        in_specs=[vmem, vmem],
        out_specs=(hbm, hbm),
        scratch_shapes=[pltpu.SemaphoreType.DMA((2,))],
        name="write",
    )(*[pltpu.with_memory_space_constraint(r, pltpu.VMEM) for r in results])


def solution(mesh):
    placed = (
        P(None, None, "gx", "gy", None),
        P(None, "gx", "gy", None),
        P(None, "gx", "gy", None),
        P("gx", "gy", None),
        P(),
    )
    return jax.shard_map(
        functools.partial(shards, mesh.shape["gx"], mesh.shape["gy"]),
        mesh=mesh,
        in_specs=placed,
        out_specs=(P(None, "gx", "gy", None), P()),
        check_vma=False,
    )
```
